32 devices in a mesh: seq: 2 (over x), tensor: 4 (over y, core), dp: 4 (over z).
Axes of the slice: x: 2, y: 2, z: 4, core: 2. Of those that a mesh axis runs over, the one named last changes fastest.
Arguments:
- inputs: bfloat16 [4, 512, 3584], P('dp', 'seq'), may hold values from -6 to 6
- w_query: bfloat16 [3584, 2048], P(('seq', 'dp'), 'tensor'), may hold values from -0.09375 to 0.09375
- w_key: bfloat16 [3584, 1024], P(('seq', 'dp'), 'tensor'), may hold values from -0.09375 to 0.09375
- w_value: bfloat16 [3584, 1024], P(('seq', 'dp'), 'tensor'), may hold values from -0.09375 to 0.09375
- norm_gain: float32 [3584], replicated, may hold values from 0.1 to 1.9
- attn_grad: bfloat16 [4, 512, 2048], P('dp', 'seq', 'tensor'), may hold values from -200 to 200
Outputs:
- grad_query: float32 [3584, 2048], P(('seq', 'dp'), 'tensor')
- grad_key: float32 [3584, 1024], P(('seq', 'dp'), 'tensor')
- grad_value: float32 [3584, 1024], P(('seq', 'dp'), 'tensor')
- input_grad: bfloat16 [4, 512, 3584], P('dp', 'seq', 'tensor')
The draws below stay inside these ranges and needn't reach their ends.
All inputs are finite; a program needn't handle non-finite values.
Results may differ from the reference program's by a relative error of at most 0.01.
Values may be sent and summed in bfloat16 or wider, within the bound.
A program may use at most 64 MiB of HBM per device.

```python
import math
import jax
import jax.numpy as jnp
from jax import lax

D = 3584
H = 8
KVH = 4
HD = 256
TOK_DEV = 256
LENGTH = 512
WINDOW = 256
EXAMPLES = 4


def draw_attn_grad(key, part):
    split_keys = jax.random.split(jax.random.fold_in(key, 17), 3)
    full_shape = (EXAMPLES, LENGTH, H * HD)
    base_draw = jnp.clip(jax.random.normal(split_keys[0], full_shape, jnp.float32), -4.0, 4.0)
    row_scale = jnp.exp(jax.random.uniform(split_keys[1], (EXAMPLES, LENGTH, 1), jnp.float32, math.log(0.3), math.log(3.0)))
    rising = 1.0 + 2.0 * jnp.arange(LENGTH).astype(jnp.float32)[None, :, None] / (LENGTH - 1)
    col_scale = jnp.exp(jax.random.uniform(split_keys[2], (1, 1, H * HD), jnp.float32, math.log(0.3), math.log(3.0)))
    return (base_draw * row_scale * rising * col_scale).astype(jnp.bfloat16)


def block_scale(key, shape, shards, smallest, top_value):
    def one(axis_at, blocks):
        steps = jax.random.uniform(jax.random.fold_in(jax.random.fold_in(key, 6), axis_at), (blocks,), jnp.float32, smallest / len(shards), top_value / len(shards))
        return jnp.repeat(jnp.exp(steps), shape[axis_at] // blocks).reshape((-1,) + (1,) * (len(shape) - axis_at - 1))

    level = one(*shards[0])
    for cut in shards[1:]:
        level = level * one(*cut)
    return level


def centred(key, dims, scale, bound, cuts=(), kind=jnp.bfloat16):
    entries = scale * jax.random.normal(key, dims, jnp.float32)
    if cuts:
        entries = entries * block_scale(key, dims, cuts, -0.22, 0.18)
    return jnp.clip(entries, -bound, bound).astype(kind)


def setup_inputs(seed: int = 0) -> dict:
    key_of = jax.random.split(jax.random.key(seed), 7)
    return {
        "inputs": centred(key_of[0], (EXAMPLES, LENGTH, D), 1.0, 6.0, ((0, 4), (1, 2))),
        "w_query": centred(key_of[1], (D, H * HD), D ** -0.5, 0.09375, ((0, 8), (1, 4))),
        "w_key": centred(key_of[2], (D, KVH * HD), D ** -0.5, 0.09375, ((0, 8), (1, 4))),
        "w_value": centred(key_of[3], (D, KVH * HD), D ** -0.5, 0.09375, ((0, 8), (1, 4))),
        "norm_gain": jnp.clip(1.0 + 0.18 * jax.random.normal(key_of[4], (D,), jnp.float32), 0.1, 1.9),
        "attn_grad": draw_attn_grad(jax.random.fold_in(key_of[6], 71), 0),
    }


EPSILON = 1e-06
SOFTCAP = 50.0
CLIP_BOUND = 1.0
ROPE_BASE = 10000.0

def angles(positions, head_width):
    frequency = ROPE_BASE ** (-2.0 * jnp.arange(head_width // 2).astype(jnp.float32) / head_width)
    phases = positions.astype(jnp.float32)[:, None] * frequency[None, :]
    return (jnp.cos(phases)[:, None, :], jnp.sin(phases)[:, None, :])

def rotate(vectors, cosine, sine_part, direction):
    half_width = vectors.shape[-1] // 2
    first_half = vectors[..., :half_width]
    second_half = vectors[..., half_width:]
    return jnp.concatenate([first_half * cosine - direction * second_half * sine_part, second_half * cosine + direction * first_half * sine_part], -1)

def attend(queries, key_rows, value_rows, query_pos, key_pos, cotangent):
    query_count, head_count, head_width = queries.shape
    kv_heads = key_rows.shape[1]
    group_size = head_count // kv_heads
    grouped_query = queries.reshape(query_count, kv_heads, group_size, head_width).astype(jnp.float32)
    grouped_cot = cotangent.reshape(query_count, kv_heads, group_size, head_width).astype(jnp.float32)
    key_float = key_rows.astype(jnp.float32)
    value_float = value_rows.astype(jnp.float32)
    inv_scale = 1.0 / math.sqrt(head_width)
    logits = jnp.einsum('tkgd,skd->kgts', grouped_query, key_float) * inv_scale
    squash = jnp.tanh(logits / SOFTCAP)
    allowed = (key_pos[None, :] <= query_pos[:, None]) & (key_pos[None, :] > query_pos[:, None] - WINDOW) & (key_pos[None, :] >= 0)
    exp_terms = jnp.where(allowed, jnp.exp(SOFTCAP * squash), 0.0)
    softmax = exp_terms / lax.optimization_barrier(jnp.sum(exp_terms, -1, keepdims=True))
    probs_low = softmax.astype(jnp.bfloat16).astype(jnp.float32)
    dsoftmax = jnp.einsum('tkgd,skd->kgts', grouped_cot, value_float)
    value_grads = jnp.einsum('kgts,tkgd->skd', probs_low, grouped_cot)
    row_delta = lax.optimization_barrier(jnp.sum(softmax * dsoftmax, -1, keepdims=True))
    dlogits = (softmax * (dsoftmax - row_delta) * (1.0 - squash * squash) * inv_scale).astype(jnp.bfloat16).astype(jnp.float32)
    dquery = jnp.einsum('kgts,skd->tkgd', dlogits, key_float).reshape(query_count, head_count, head_width)
    key_grads = jnp.einsum('kgts,tkgd->skd', dlogits, grouped_query)
    return (dquery, key_grads, value_grads)

def example_terms(inputs_one, w_all, norm_gain, cot_one):
    seq_len = inputs_one.shape[0]
    width_q = H * HD
    width_k = KVH * HD
    widened = inputs_one.astype(jnp.float32)
    inverse_rms = lax.rsqrt(lax.optimization_barrier(jnp.mean(widened * widened, -1)) + EPSILON)
    normed = (widened * inverse_rms[:, None] * norm_gain[None, :]).astype(jnp.bfloat16)
    projected = jnp.dot(normed, w_all, preferred_element_type=jnp.float32)
    positions = jnp.arange(seq_len, dtype=jnp.int32)
    cosine, sine_part = angles(positions, HD)
    rotated_query = rotate(projected[:, :width_q].reshape(seq_len, H, HD), cosine, sine_part, 1.0).astype(jnp.bfloat16)
    rotated_keys = rotate(projected[:, width_q:width_q + width_k].reshape(seq_len, KVH, HD), cosine, sine_part, 1.0).astype(jnp.bfloat16)
    value_rows = projected[:, width_q + width_k:].reshape(seq_len, KVH, HD).astype(jnp.bfloat16)
    block_count = seq_len // TOK_DEV
    query_blocks = rotated_query.reshape(block_count, TOK_DEV, H, HD)
    key_blocks = rotated_keys.reshape(block_count, TOK_DEV, KVH, HD)
    value_blocks = value_rows.reshape(block_count, TOK_DEV, KVH, HD)
    zero_block = jnp.zeros_like(key_blocks[:1])
    key_ext = jnp.concatenate([jnp.concatenate([zero_block, key_blocks[:-1]], 0), key_blocks], 1)
    value_ext = jnp.concatenate([jnp.concatenate([zero_block, value_blocks[:-1]], 0), value_blocks], 1)
    cot_blocks = cot_one.reshape(block_count, TOK_DEV, H * HD)
    block_starts = jnp.arange(block_count, dtype=jnp.int32) * TOK_DEV

    def one_block(block_args):
        query_b, key_b, value_b, cot_b, first_row = block_args
        query_pos = first_row + jnp.arange(TOK_DEV, dtype=jnp.int32)
        key_pos = first_row - TOK_DEV + jnp.arange(2 * TOK_DEV, dtype=jnp.int32)
        return attend(query_b, key_b, value_b, query_pos, key_pos, cot_b)
    dquery, key_ext_grad, value_ext_grad = lax.map(one_block, (query_blocks, key_ext, value_ext, cot_blocks, block_starts))
    zero_grad = jnp.zeros_like(key_ext_grad[:1, :TOK_DEV])
    key_grads = key_ext_grad[:, TOK_DEV:] + jnp.concatenate([key_ext_grad[1:, :TOK_DEV], zero_grad], 0)
    value_grads = value_ext_grad[:, TOK_DEV:] + jnp.concatenate([value_ext_grad[1:, :TOK_DEV], zero_grad], 0)
    dquery = rotate(dquery.reshape(seq_len, H, HD), cosine, sine_part, -1.0)
    key_grads = rotate(key_grads.reshape(seq_len, KVH, HD), cosine, sine_part, -1.0)
    d_out = jnp.concatenate([dquery.reshape(seq_len, width_q), key_grads.reshape(seq_len, width_k), value_grads.reshape(seq_len, width_k)], 1).astype(jnp.bfloat16)
    example_grad = jnp.dot(normed.T, d_out, preferred_element_type=jnp.float32)
    dnormed = lax.dot_general(d_out, w_all, (((1,), (1,)), ((), ())), preferred_element_type=jnp.float32)
    scaled = norm_gain[None, :] * dnormed
    mean_term = lax.optimization_barrier(jnp.mean(widened * scaled, -1, keepdims=True))
    input_grad = (inverse_rms[:, None] * scaled - widened * (inverse_rms ** 3)[:, None] * mean_term).astype(jnp.bfloat16)
    return (example_grad, input_grad)

def reference(inputs, w_query, w_key, w_value, norm_gain, attn_grad):
    width_q = H * HD
    width_k = KVH * HD
    w_all = jnp.concatenate([w_query, w_key, w_value], 1)
    entry_count = D * (H + 2 * KVH) * HD

    def step_example(summed, example_args):
        inputs_one, cot_one = example_args
        example_grad, input_grad = example_terms(inputs_one, w_all, norm_gain, cot_one)
        grad_rms = jnp.sqrt(jnp.sum(example_grad * example_grad) / entry_count + EPSILON)
        factor = CLIP_BOUND / jnp.maximum(grad_rms, CLIP_BOUND)
        return (summed + factor * example_grad, input_grad)
    summed, input_grad = lax.scan(step_example, jnp.zeros((D, w_all.shape[1]), jnp.float32), (inputs, attn_grad))
    return (summed[:, :width_q], summed[:, width_q:width_q + width_k], summed[:, width_q + width_k:], input_grad)
```

```python
import functools
import math

import jax
import jax.numpy as jnp
from jax import lax
from jax.experimental import pallas as pl
from jax.experimental.pallas import tpu as pltpu
from jax.sharding import PartitionSpec as P

D = 3584
H = 8
KVH = 4
HD = 256
WINDOW = 256


EPSILON = 1e-06
SOFTCAP = 50.0
CLIP_BOUND = 1.0
ROPE_BASE = 10000.0


def shifted(value, axis, steps):
    count = lax.axis_size(axis)
    leading, last = (max(0, -steps), min(count, count - steps))
    return lax.ppermute(value, axis, [(source, source + steps) for source in range(leading, last)])


def angles(positions, head_width):
    frequency = ROPE_BASE ** (-2.0 * jnp.arange(head_width // 2).astype(jnp.float32) / head_width)
    phases = positions.astype(jnp.float32)[:, None] * frequency[None, :]
    return (jnp.cos(phases)[:, None, :], jnp.sin(phases)[:, None, :])


def rotate(vectors, cosine, sine_part, direction):
    half_width = vectors.shape[-1] // 2
    first_half = vectors[..., :half_width]
    second_half = vectors[..., half_width:]
    return jnp.concatenate(
        [
            first_half * cosine - direction * second_half * sine_part,
            second_half * cosine + direction * first_half * sine_part,
        ],
        -1,
    )


def attend(queries, key_rows, value_rows, query_pos, key_pos, cotangent):
    query_count, head_count, head_width = queries.shape
    kv_heads = key_rows.shape[1]
    group_size = head_count // kv_heads
    grouped_query = queries.reshape(query_count, kv_heads, group_size, head_width)
    grouped_cot = cotangent.reshape(query_count, kv_heads, group_size, head_width)
    inv_scale = 1.0 / math.sqrt(head_width)
    logits = (
        jnp.einsum("tkgd,skd->kgts", grouped_query, key_rows, preferred_element_type=jnp.float32)
        * inv_scale
    )
    squash = jnp.tanh(logits / SOFTCAP)
    allowed = (
        (key_pos[None, :] <= query_pos[:, None])
        & (key_pos[None, :] > query_pos[:, None] - WINDOW)
        & (key_pos[None, :] >= 0)
    )
    exp_terms = jnp.where(allowed, jnp.exp(SOFTCAP * squash), 0.0)
    softmax = exp_terms / jnp.sum(exp_terms, -1, keepdims=True)
    probs_low = softmax.astype(jnp.bfloat16)
    dsoftmax = jnp.einsum(
        "tkgd,skd->kgts", grouped_cot, value_rows, preferred_element_type=jnp.float32
    )
    value_grads = jnp.einsum(
        "kgts,tkgd->skd", probs_low, grouped_cot, preferred_element_type=jnp.float32
    )
    row_delta = jnp.sum(softmax * dsoftmax, -1, keepdims=True)
    dlogits = (softmax * (dsoftmax - row_delta) * (1.0 - squash * squash) * inv_scale).astype(
        jnp.bfloat16
    )
    dquery = jnp.einsum("kgts,skd->tkgd", dlogits, key_rows, preferred_element_type=jnp.float32)
    key_grads = jnp.einsum(
        "kgts,tkgd->skd", dlogits, grouped_query, preferred_element_type=jnp.float32
    )
    return (dquery.reshape(query_count, head_count, head_width), key_grads, value_grads)


MESH = pl.DeviceIdType.MESH


def greet(axes):
    barrier = pltpu.get_barrier_semaphore()
    for axis in axes:
        count = lax.axis_size(axis)
        me = lax.axis_index(axis)
        for step in (1, -1):

            @pl.when((me + step >= 0) & (me + step < count))
            def _():
                pl.semaphore_signal(
                    barrier, inc=1, device_id={axis: me + step}, device_id_type=MESH
                )

    near = 0
    for axis in axes:
        me = lax.axis_index(axis)
        near = near + jnp.minimum(me, 1) + jnp.minimum(lax.axis_size(axis) - 1 - me, 1)
    pl.semaphore_wait(barrier, near)


class LineGather:
    def __init__(self, order, part, first, second, low, high, x_ref, out_ref, send_sem, recv_sem):
        self.order = order
        self.part, self.first, self.second = part, first, second
        self.rows = pl.ds(low, high - low)
        self.x_ref, self.out_ref = x_ref, out_ref
        self.send_sem, self.recv_sem = send_sem, recv_sem
        self.me = {axis: lax.axis_index(axis) for axis in (first, second)}
        self.count = {axis: lax.axis_size(axis) for axis in (first, second)}
        self.sends = []

    def slot(self, at):
        return self.out_ref.at[tuple(at[axis] for axis in self.order) + (self.rows,)]

    def copy(self, at, axis, step, own):
        way = (0 if axis == "seq" else 2) + (0 if step == 1 else 1)
        return pltpu.make_async_remote_copy(
            src_ref=self.x_ref.at[self.rows] if own else self.slot(at),
            dst_ref=self.slot(at),
            send_sem=self.send_sem.at[self.part, way, at["seq"], at["dp"]],
            recv_sem=self.recv_sem.at[self.part, at["seq"], at["dp"]],
            device_id={axis: self.me[axis] + step},
            device_id_type=MESH,
        )

    def inside(self, axis, value):
        return (value >= 0) & (value < self.count[axis])

    def send(self, at, axis, step, held, own=False):
        ok = held & self.inside(axis, self.me[axis] + step)

        @pl.when(ok)
        def _():
            self.copy(at, axis, step, own).start()

        self.sends.append((at, axis, step, ok, own))

    def receive(self, at, held):
        @pl.when(held)
        def _():
            self.copy(at, self.first, 1, False).wait_recv()

    def steps(self):
        first, second = self.first, self.second
        here = jnp.bool_(True)
        for axis in (first, second):
            for step in (1, -1):
                self.send(dict(self.me), axis, step, here, True)
        yield
        column = [(dict(self.me), here, True)]
        for hop in range(1, self.count[first]):
            for step in (1, -1):
                at = {**self.me, first: self.me[first] - step * hop}
                held = self.inside(first, at[first])
                self.receive(at, held)
                self.send(at, first, step, held)
                for way in (1, -1):
                    self.send(at, second, way, held)
                column.append((at, held, False))
            yield
        for hop in range(1, self.count[second]):
            for base, held_base, _ in column:
                for step in (1, -1):
                    at = {**base, second: self.me[second] - step * hop}
                    held = held_base & self.inside(second, at[second])
                    self.receive(at, held)
                    self.send(at, second, step, held)
            yield

    def finish(self):
        for at, axis, step, ok, own in self.sends:

            @pl.when(ok)
            def _():
                self.copy(at, axis, step, own).wait_send()


def run_gathers(gathers):
    live = [gather.steps() for gather in gathers]
    while live:
        still = []
        for walk in live:
            try:
                next(walk)
                still.append(walk)
            except StopIteration:
                pass
        live = still
    for gather in gathers:
        gather.finish()


def gather_kernel(cut, order, x_ref, out_ref, send_sem, recv_sem, own_sem):
    rows = x_ref.shape[0]
    own = pltpu.make_async_copy(
        x_ref, out_ref.at[tuple(lax.axis_index(axis) for axis in order)], own_sem
    )
    own.start()
    greet(("seq", "dp"))
    run_gathers(
        [
            LineGather(order, 0, "seq", "dp", 0, cut, x_ref, out_ref, send_sem, recv_sem),
            LineGather(order, 1, "dp", "seq", cut, rows, x_ref, out_ref, send_sem, recv_sem),
        ]
    )
    own.wait()


def gather_blocks(x, cut, order, collective_id):
    shape = (lax.axis_size("seq"), lax.axis_size("dp"))
    return pl.pallas_call(
        functools.partial(gather_kernel, cut, order),
        out_shape=jax.ShapeDtypeStruct(
            tuple(lax.axis_size(axis) for axis in order) + x.shape, x.dtype
        ),
        in_specs=[pl.BlockSpec(memory_space=pltpu.VMEM)],
        out_specs=pl.BlockSpec(memory_space=pl.ANY),
        scratch_shapes=[
            pltpu.SemaphoreType.DMA((2, 4) + shape),
            pltpu.SemaphoreType.DMA((2,) + shape),
            pltpu.SemaphoreType.DMA,
        ],
        compiler_params=pltpu.CompilerParams(
            collective_id=collective_id, has_side_effects=True
        ),
    )(x)


def exchange_kernel(x_ref, out_ref, send_sem, recv_sem, own_sem):
    seqs, dps = lax.axis_size("seq"), lax.axis_size("dp")
    seq, dp = lax.axis_index("seq"), lax.axis_index("dp")
    barrier = pltpu.get_barrier_semaphore()
    own = pltpu.make_async_copy(x_ref.at[seq, dp], out_ref.at[dp, seq], own_sem)
    own.start()
    peers = []
    for ds in range(seqs):
        for dd in range(dps):
            if ds or dd:
                peers.append((lax.rem(seq + ds, seqs), lax.rem(dp + dd, dps)))
    for s, d in peers:
        pl.semaphore_signal(
            barrier, inc=1, device_id={"seq": s, "dp": d}, device_id_type=MESH
        )
    pl.semaphore_wait(barrier, len(peers))
    for s, d in peers:
        pltpu.make_async_remote_copy(
            src_ref=x_ref.at[s, d],
            dst_ref=out_ref.at[dp, seq],
            send_sem=send_sem.at[s, d],
            recv_sem=recv_sem.at[seq, dp],
            device_id={"seq": s, "dp": d},
            device_id_type=MESH,
        ).start()
    for s, d in peers:
        pltpu.make_async_remote_copy(
            src_ref=x_ref.at[s, d],
            dst_ref=out_ref.at[d, s],
            send_sem=send_sem.at[s, d],
            recv_sem=recv_sem.at[s, d],
            device_id={"seq": s, "dp": d},
            device_id_type=MESH,
        ).wait()
    own.wait()


def exchange_blocks(x, collective_id):
    shape = x.shape[:2]
    return pl.pallas_call(
        exchange_kernel,
        out_shape=jax.ShapeDtypeStruct((shape[1], shape[0]) + x.shape[2:], x.dtype),
        in_specs=[pl.BlockSpec(memory_space=pltpu.VMEM)],
        out_specs=pl.BlockSpec(memory_space=pl.ANY),
        scratch_shapes=[
            pltpu.SemaphoreType.DMA(shape),
            pltpu.SemaphoreType.DMA(shape),
            pltpu.SemaphoreType.DMA,
        ],
        compiler_params=pltpu.CompilerParams(
            collective_id=collective_id, has_side_effects=True
        ),
    )(x)


def cut_of(rows):
    return max(16, rows // 7 // 16 * 16)


def local(inputs, w_query, w_key, w_value, norm_gain, attn_grad):
    widened = inputs[0].astype(jnp.float32)
    row_count = widened.shape[0]
    inverse_rms = lax.rsqrt(jnp.mean(widened * widened, -1) + EPSILON)
    normed = (widened * inverse_rms[:, None] * norm_gain[None, :]).astype(jnp.bfloat16)
    width_q = w_query.shape[1]
    width_k = w_key.shape[1]
    local_w = jnp.concatenate([w_query, w_key, w_value], 1)
    seqs, dps = lax.axis_size("seq"), lax.axis_size("dp")
    rows_w = local_w.shape[0]
    full_w = gather_blocks(local_w, cut_of(rows_w), ("seq", "dp"), 0).reshape(seqs * dps * rows_w, -1)
    slabs = exchange_blocks(normed.T.reshape(seqs, dps, rows_w, row_count), 1)
    projected = jnp.dot(normed, full_w, preferred_element_type=jnp.float32)
    start_row = lax.axis_index("seq") * row_count
    query_pos = start_row + jnp.arange(row_count, dtype=jnp.int32)
    key_pos = start_row - row_count + jnp.arange(2 * row_count, dtype=jnp.int32)
    cosine, sine_part = angles(query_pos, HD)
    heads_q = width_q // HD
    heads_k = width_k // HD
    rotated_query = rotate(
        projected[:, :width_q].reshape(row_count, heads_q, HD), cosine, sine_part, 1.0
    ).astype(jnp.bfloat16)
    rotated_keys = rotate(
        projected[:, width_q : width_q + width_k].reshape(row_count, heads_k, HD),
        cosine,
        sine_part,
        1.0,
    ).astype(jnp.bfloat16)
    value_rows = (
        projected[:, width_q + width_k :].reshape(row_count, heads_k, HD).astype(jnp.bfloat16)
    )
    keys_before, values_before = shifted((rotated_keys, value_rows), "seq", 1)
    dquery, key_ext_grad, value_ext_grad = attend(
        rotated_query,
        jnp.concatenate([keys_before, rotated_keys], 0),
        jnp.concatenate([values_before, value_rows], 0),
        query_pos,
        key_pos,
        attn_grad[0],
    )
    back_keys, back_values = shifted(
        (key_ext_grad[:row_count], value_ext_grad[:row_count]), "seq", -1
    )
    key_grads = key_ext_grad[row_count:] + back_keys
    value_grads = value_ext_grad[row_count:] + back_values
    dquery = rotate(dquery, cosine, sine_part, -1.0)
    key_grads = rotate(key_grads, cosine, sine_part, -1.0)
    d_out = jnp.concatenate(
        [
            dquery.reshape(row_count, width_q),
            key_grads.reshape(row_count, width_k),
            value_grads.reshape(row_count, width_k),
        ],
        1,
    ).astype(jnp.bfloat16)
    cotangents = gather_blocks(d_out, cut_of(row_count), ("dp", "seq"), 2)
    grads = []
    for example in range(dps):
        grads.append(
            sum(
                jnp.dot(
                    slabs[example, s], cotangents[example, s], preferred_element_type=jnp.float32
                )
                for s in range(seqs)
            )
        )
    square_sum = lax.psum(
        jnp.stack([jnp.sum(grad * grad) for grad in grads]), ("seq", "tensor", "dp")
    )
    grad_rms = jnp.sqrt(square_sum / (D * (H + 2 * KVH) * HD) + EPSILON)
    factor = CLIP_BOUND / jnp.maximum(grad_rms, CLIP_BOUND)
    clipped = sum(factor[example] * grads[example] for example in range(dps))
    dnormed = lax.dot_general(
        d_out, full_w, (((1,), (1,)), ((), ())), preferred_element_type=jnp.float32
    )
    part_width = D // lax.axis_size("tensor")
    offset = lax.axis_index("tensor") * part_width
    part_grad = lax.psum_scatter(dnormed, "tensor", scatter_dimension=1, tiled=True)
    gain_slab = lax.dynamic_slice_in_dim(norm_gain, offset, part_width, 0)
    input_slab = lax.dynamic_slice_in_dim(widened, offset, part_width, 1)
    scaled = gain_slab[None, :] * part_grad
    inner_sum = lax.psum(jnp.sum(input_slab * scaled, -1), "tensor")
    mean_term = (inner_sum / D)[:, None]
    input_grad = (
        inverse_rms[:, None] * scaled
        - input_slab * (inverse_rms * inverse_rms * inverse_rms)[:, None] * mean_term
    )
    return (
        clipped[:, :width_q],
        clipped[:, width_q : width_q + width_k],
        clipped[:, width_q + width_k :],
        input_grad.astype(jnp.bfloat16)[None],
    )


def solution(mesh):
    return jax.shard_map(
        local,
        mesh=mesh,
        in_specs=(
            P("dp", "seq", None),
            P(("seq", "dp"), "tensor"),
            P(("seq", "dp"), "tensor"),
            P(("seq", "dp"), "tensor"),
            P(),
            P("dp", "seq", "tensor"),
        ),
        out_specs=(
            P(("seq", "dp"), "tensor"),
            P(("seq", "dp"), "tensor"),
            P(("seq", "dp"), "tensor"),
            P("dp", "seq", "tensor"),
        ),
        check_vma=False,
    )
```

```python
import functools
import math

import jax
import jax.numpy as jnp
from jax import lax
from jax.experimental import pallas as pl
from jax.experimental.pallas import tpu as pltpu
from jax.sharding import PartitionSpec as P

D = 3584
H = 8
KVH = 4
HD = 256
WINDOW = 256


EPSILON = 1e-06
SOFTCAP = 50.0
CLIP_BOUND = 1.0
ROPE_BASE = 10000.0


def shifted(value, axis, steps):
    count = lax.axis_size(axis)
    leading, last = (max(0, -steps), min(count, count - steps))
    return lax.ppermute(value, axis, [(source, source + steps) for source in range(leading, last)])


def angles(positions, head_width):
    frequency = ROPE_BASE ** (-2.0 * jnp.arange(head_width // 2).astype(jnp.float32) / head_width)
    phases = positions.astype(jnp.float32)[:, None] * frequency[None, :]
    return (jnp.cos(phases)[:, None, :], jnp.sin(phases)[:, None, :])


def rotate(vectors, cosine, sine_part, direction):
    half_width = vectors.shape[-1] // 2
    first_half = vectors[..., :half_width]
    second_half = vectors[..., half_width:]
    return jnp.concatenate(
        [
            first_half * cosine - direction * second_half * sine_part,
            second_half * cosine + direction * first_half * sine_part,
        ],
        -1,
    )


def attend(queries, key_rows, value_rows, query_pos, key_pos, cotangent):
    query_count, head_count, head_width = queries.shape
    kv_heads = key_rows.shape[1]
    group_size = head_count // kv_heads
    grouped_query = queries.reshape(query_count, kv_heads, group_size, head_width)
    grouped_cot = cotangent.reshape(query_count, kv_heads, group_size, head_width)
    inv_scale = 1.0 / math.sqrt(head_width)
    logits = (
        jnp.einsum("tkgd,skd->kgts", grouped_query, key_rows, preferred_element_type=jnp.float32)
        * inv_scale
    )
    squash = jnp.tanh(logits / SOFTCAP)
    allowed = (
        (key_pos[None, :] <= query_pos[:, None])
        & (key_pos[None, :] > query_pos[:, None] - WINDOW)
        & (key_pos[None, :] >= 0)
    )
    exp_terms = jnp.where(allowed, jnp.exp(SOFTCAP * squash), 0.0)
    softmax = exp_terms / jnp.sum(exp_terms, -1, keepdims=True)
    probs_low = softmax.astype(jnp.bfloat16)
    dsoftmax = jnp.einsum(
        "tkgd,skd->kgts", grouped_cot, value_rows, preferred_element_type=jnp.float32
    )
    value_grads = jnp.einsum(
        "kgts,tkgd->skd", probs_low, grouped_cot, preferred_element_type=jnp.float32
    )
    row_delta = jnp.sum(softmax * dsoftmax, -1, keepdims=True)
    dlogits = (softmax * (dsoftmax - row_delta) * (1.0 - squash * squash) * inv_scale).astype(
        jnp.bfloat16
    )
    dquery = jnp.einsum("kgts,skd->tkgd", dlogits, key_rows, preferred_element_type=jnp.float32)
    key_grads = jnp.einsum(
        "kgts,tkgd->skd", dlogits, grouped_query, preferred_element_type=jnp.float32
    )
    return (dquery.reshape(query_count, head_count, head_width), key_grads, value_grads)


MESH = pl.DeviceIdType.MESH


def greet(axes, peers=()):
    barrier = pltpu.get_barrier_semaphore()
    for axis in axes:
        count = lax.axis_size(axis)
        me = lax.axis_index(axis)
        for step in (1, -1):

            @pl.when((me + step >= 0) & (me + step < count))
            def _():
                pl.semaphore_signal(
                    barrier, inc=1, device_id={axis: me + step}, device_id_type=MESH
                )

    for peer in peers:
        pl.semaphore_signal(barrier, inc=1, device_id=peer, device_id_type=MESH)
    near = len(peers)
    for axis in axes:
        me = lax.axis_index(axis)
        near = near + jnp.minimum(me, 1) + jnp.minimum(lax.axis_size(axis) - 1 - me, 1)
    pl.semaphore_wait(barrier, near)


class LineGather:
    def __init__(self, order, part, first, second, low, high, x_ref, out_ref, send_sem, recv_sem):
        self.order = order
        self.part, self.first, self.second = part, first, second
        self.rows = pl.ds(low, high - low)
        self.x_ref, self.out_ref = x_ref, out_ref
        self.send_sem, self.recv_sem = send_sem, recv_sem
        self.me = {axis: lax.axis_index(axis) for axis in (first, second)}
        self.count = {axis: lax.axis_size(axis) for axis in (first, second)}
        self.sends = []

    def slot(self, at):
        return self.out_ref.at[tuple(at[axis] for axis in self.order) + (self.rows,)]

    def copy(self, at, axis, step, own):
        way = (0 if axis == "seq" else 2) + (0 if step == 1 else 1)
        return pltpu.make_async_remote_copy(
            src_ref=self.x_ref.at[self.rows] if own else self.slot(at),
            dst_ref=self.slot(at),
            send_sem=self.send_sem.at[self.part, way, at["seq"], at["dp"]],
            recv_sem=self.recv_sem.at[self.part, at["seq"], at["dp"]],
            device_id={axis: self.me[axis] + step},
            device_id_type=MESH,
        )

    def inside(self, axis, value):
        return (value >= 0) & (value < self.count[axis])

    def send(self, at, axis, step, held, own=False):
        ok = held & self.inside(axis, self.me[axis] + step)

        @pl.when(ok)
        def _():
            self.copy(at, axis, step, own).start()

        self.sends.append((at, axis, step, ok, own))

    def receive(self, at, held):
        @pl.when(held)
        def _():
            self.copy(at, self.first, 1, False).wait_recv()

    def steps(self):
        first, second = self.first, self.second
        here = jnp.bool_(True)
        for axis in (first, second):
            for step in (1, -1):
                self.send(dict(self.me), axis, step, here, True)
        yield
        column = [(dict(self.me), here, True)]
        for hop in range(1, self.count[first]):
            for step in (1, -1):
                at = {**self.me, first: self.me[first] - step * hop}
                held = self.inside(first, at[first])
                self.receive(at, held)
                self.send(at, first, step, held)
                for way in (1, -1):
                    self.send(at, second, way, held)
                column.append((at, held, False))
            yield
        for hop in range(1, self.count[second]):
            for base, held_base, _ in column:
                for step in (1, -1):
                    at = {**base, second: self.me[second] - step * hop}
                    held = held_base & self.inside(second, at[second])
                    self.receive(at, held)
                    self.send(at, second, step, held)
            yield

    def finish(self):
        for at, axis, step, ok, own in self.sends:

            @pl.when(ok)
            def _():
                self.copy(at, axis, step, own).wait_send()


def run_gathers(gathers):
    live = [gather.steps() for gather in gathers]
    while live:
        still = []
        for walk in live:
            try:
                next(walk)
                still.append(walk)
            except StopIteration:
                pass
        live = still
    for gather in gathers:
        gather.finish()


def gather_kernel(cut, order, x_ref, out_ref, send_sem, recv_sem, own_sem):
    rows = x_ref.shape[0]
    own = pltpu.make_async_copy(
        x_ref, out_ref.at[tuple(lax.axis_index(axis) for axis in order)], own_sem
    )
    own.start()
    greet(("seq", "dp"))
    run_gathers(
        [
            LineGather(order, 0, "seq", "dp", 0, cut, x_ref, out_ref, send_sem, recv_sem),
            LineGather(order, 1, "dp", "seq", cut, rows, x_ref, out_ref, send_sem, recv_sem),
        ]
    )
    own.wait()


def gather_blocks(x, cut, order, collective_id):
    shape = (lax.axis_size("seq"), lax.axis_size("dp"))
    return pl.pallas_call(
        functools.partial(gather_kernel, cut, order),
        out_shape=jax.ShapeDtypeStruct(
            tuple(lax.axis_size(axis) for axis in order) + x.shape, x.dtype
        ),
        in_specs=[pl.BlockSpec(memory_space=pltpu.VMEM)],
        out_specs=pl.BlockSpec(memory_space=pl.ANY),
        scratch_shapes=[
            pltpu.SemaphoreType.DMA((2, 4) + shape),
            pltpu.SemaphoreType.DMA((2,) + shape),
            pltpu.SemaphoreType.DMA,
        ],
        compiler_params=pltpu.CompilerParams(
            collective_id=collective_id, has_side_effects=True
        ),
    )(x)


def tail_kernel(
    cut,
    order,
    x_ref,
    part_ref,
    inner_ref,
    out_ref,
    parts_ref,
    inners_ref,
    send_sem,
    recv_sem,
    own_sem,
    part_send,
    part_recv,
    inner_send,
    inner_recv,
):
    rows = x_ref.shape[0]
    count, me = lax.axis_size("tensor"), lax.axis_index("tensor")
    width = part_ref.shape[1] // count

    def slab(index):
        return part_ref.at[:, pl.ds(pl.multiple_of(index * width, 128), width)]

    owns = [
        pltpu.make_async_copy(
            x_ref, out_ref.at[tuple(lax.axis_index(axis) for axis in order)], own_sem.at[0]
        ),
        pltpu.make_async_copy(slab(me), parts_ref.at[me], own_sem.at[1]),
        pltpu.make_async_copy(inner_ref, inners_ref.at[me], own_sem.at[2]),
    ]
    for own in owns:
        own.start()
    others = [lax.rem(me + hop, count) for hop in range(1, count)]
    greet(("seq", "dp"), [{"tensor": other} for other in others])
    copies = []
    for index, other in enumerate(others):
        copies.append(
            pltpu.make_async_remote_copy(
                src_ref=slab(other),
                dst_ref=parts_ref.at[me],
                send_sem=part_send.at[index],
                recv_sem=part_recv.at[index],
                device_id={"tensor": other},
                device_id_type=MESH,
            )
        )
        copies.append(
            pltpu.make_async_remote_copy(
                src_ref=inner_ref,
                dst_ref=inners_ref.at[me],
                send_sem=inner_send.at[index],
                recv_sem=inner_recv.at[index],
                device_id={"tensor": other},
                device_id_type=MESH,
            )
        )
    for copy in copies:
        copy.start()
    run_gathers(
        [
            LineGather(order, 0, "seq", "dp", 0, cut, x_ref, out_ref, send_sem, recv_sem),
            LineGather(order, 1, "dp", "seq", cut, rows, x_ref, out_ref, send_sem, recv_sem),
        ]
    )
    for copy in copies:
        copy.wait()
    for own in owns:
        own.wait()


def gather_and_scatter(x, part, inner, cut, order, collective_id):
    shape = (lax.axis_size("seq"), lax.axis_size("dp"))
    count = lax.axis_size("tensor")
    return pl.pallas_call(
        functools.partial(tail_kernel, cut, order),
        out_shape=(
            jax.ShapeDtypeStruct(tuple(lax.axis_size(axis) for axis in order) + x.shape, x.dtype),
            jax.ShapeDtypeStruct((count, part.shape[0], part.shape[1] // count), part.dtype),
            jax.ShapeDtypeStruct((count,) + inner.shape, inner.dtype),
        ),
        in_specs=[pl.BlockSpec(memory_space=pltpu.VMEM)] * 3,
        out_specs=(pl.BlockSpec(memory_space=pl.ANY),) * 3,
        scratch_shapes=[
            pltpu.SemaphoreType.DMA((2, 4) + shape),
            pltpu.SemaphoreType.DMA((2,) + shape),
            pltpu.SemaphoreType.DMA((3,)),
        ]
        + [pltpu.SemaphoreType.DMA((count - 1,))] * 4,
        compiler_params=pltpu.CompilerParams(
            collective_id=collective_id, has_side_effects=True
        ),
    )(x, part, inner)


def exchange_kernel(x_ref, out_ref, send_sem, recv_sem, own_sem):
    seqs, dps = lax.axis_size("seq"), lax.axis_size("dp")
    seq, dp = lax.axis_index("seq"), lax.axis_index("dp")
    barrier = pltpu.get_barrier_semaphore()
    own = pltpu.make_async_copy(x_ref.at[seq, dp], out_ref.at[dp, seq], own_sem)
    own.start()
    peers = []
    for ds in range(seqs):
        for dd in range(dps):
            if ds or dd:
                peers.append((lax.rem(seq + ds, seqs), lax.rem(dp + dd, dps)))
    for s, d in peers:
        pl.semaphore_signal(
            barrier, inc=1, device_id={"seq": s, "dp": d}, device_id_type=MESH
        )
    pl.semaphore_wait(barrier, len(peers))
    for s, d in peers:
        pltpu.make_async_remote_copy(
            src_ref=x_ref.at[s, d],
            dst_ref=out_ref.at[dp, seq],
            send_sem=send_sem.at[s, d],
            recv_sem=recv_sem.at[seq, dp],
            device_id={"seq": s, "dp": d},
            device_id_type=MESH,
        ).start()
    for s, d in peers:
        pltpu.make_async_remote_copy(
            src_ref=x_ref.at[s, d],
            dst_ref=out_ref.at[d, s],
            send_sem=send_sem.at[s, d],
            recv_sem=recv_sem.at[s, d],
            device_id={"seq": s, "dp": d},
            device_id_type=MESH,
        ).wait()
    own.wait()


def exchange_blocks(x, collective_id):
    shape = x.shape[:2]
    return pl.pallas_call(
        exchange_kernel,
        out_shape=jax.ShapeDtypeStruct((shape[1], shape[0]) + x.shape[2:], x.dtype),
        in_specs=[pl.BlockSpec(memory_space=pltpu.VMEM)],
        out_specs=pl.BlockSpec(memory_space=pl.ANY),
        scratch_shapes=[
            pltpu.SemaphoreType.DMA(shape),
            pltpu.SemaphoreType.DMA(shape),
            pltpu.SemaphoreType.DMA,
        ],
        compiler_params=pltpu.CompilerParams(
            collective_id=collective_id, has_side_effects=True
        ),
    )(x)


def cut_of(rows):
    return max(16, rows // 7 // 16 * 16)


def local(inputs, w_query, w_key, w_value, norm_gain, attn_grad):
    widened = inputs[0].astype(jnp.float32)
    row_count = widened.shape[0]
    inverse_rms = lax.rsqrt(jnp.mean(widened * widened, -1) + EPSILON)
    normed = (widened * inverse_rms[:, None] * norm_gain[None, :]).astype(jnp.bfloat16)
    width_q = w_query.shape[1]
    width_k = w_key.shape[1]
    local_w = jnp.concatenate([w_query, w_key, w_value], 1)
    seqs, dps = lax.axis_size("seq"), lax.axis_size("dp")
    rows_w = local_w.shape[0]
    full_w = gather_blocks(local_w, cut_of(rows_w), ("seq", "dp"), 0).reshape(seqs * dps * rows_w, -1)
    slabs = exchange_blocks(normed.T.reshape(seqs, dps, rows_w, row_count), 1)
    projected = jnp.dot(normed, full_w, preferred_element_type=jnp.float32)
    start_row = lax.axis_index("seq") * row_count
    query_pos = start_row + jnp.arange(row_count, dtype=jnp.int32)
    key_pos = start_row - row_count + jnp.arange(2 * row_count, dtype=jnp.int32)
    cosine, sine_part = angles(query_pos, HD)
    heads_q = width_q // HD
    heads_k = width_k // HD
    rotated_query = rotate(
        projected[:, :width_q].reshape(row_count, heads_q, HD), cosine, sine_part, 1.0
    ).astype(jnp.bfloat16)
    rotated_keys = rotate(
        projected[:, width_q : width_q + width_k].reshape(row_count, heads_k, HD),
        cosine,
        sine_part,
        1.0,
    ).astype(jnp.bfloat16)
    value_rows = (
        projected[:, width_q + width_k :].reshape(row_count, heads_k, HD).astype(jnp.bfloat16)
    )
    keys_before, values_before = shifted((rotated_keys, value_rows), "seq", 1)
    dquery, key_ext_grad, value_ext_grad = attend(
        rotated_query,
        jnp.concatenate([keys_before, rotated_keys], 0),
        jnp.concatenate([values_before, value_rows], 0),
        query_pos,
        key_pos,
        attn_grad[0],
    )
    back_keys, back_values = shifted(
        (key_ext_grad[:row_count], value_ext_grad[:row_count]), "seq", -1
    )
    key_grads = key_ext_grad[row_count:] + back_keys
    value_grads = value_ext_grad[row_count:] + back_values
    dquery = rotate(dquery, cosine, sine_part, -1.0)
    key_grads = rotate(key_grads, cosine, sine_part, -1.0)
    d_out = jnp.concatenate(
        [
            dquery.reshape(row_count, width_q),
            key_grads.reshape(row_count, width_k),
            value_grads.reshape(row_count, width_k),
        ],
        1,
    ).astype(jnp.bfloat16)
    dnormed = lax.dot_general(
        d_out, full_w, (((1,), (1,)), ((), ())), preferred_element_type=jnp.float32
    )
    inner = jnp.sum(widened * norm_gain[None, :] * dnormed, -1).reshape(-1, 128)
    cotangents, parts, inners = gather_and_scatter(
        d_out, dnormed.astype(jnp.bfloat16), inner, cut_of(row_count), ("dp", "seq"), 2
    )
    grads = []
    for example in range(dps):
        grads.append(
            sum(
                jnp.dot(
                    slabs[example, s], cotangents[example, s], preferred_element_type=jnp.float32
                )
                for s in range(seqs)
            )
        )
    square_sum = lax.psum(
        jnp.stack([jnp.sum(grad * grad) for grad in grads]), ("seq", "tensor", "dp")
    )
    grad_rms = jnp.sqrt(square_sum / (D * (H + 2 * KVH) * HD) + EPSILON)
    factor = CLIP_BOUND / jnp.maximum(grad_rms, CLIP_BOUND)
    clipped = sum(factor[example] * grads[example] for example in range(dps))
    part_width = D // lax.axis_size("tensor")
    offset = lax.axis_index("tensor") * part_width
    part_grad = jnp.sum(parts.astype(jnp.float32), 0)
    gain_slab = lax.dynamic_slice_in_dim(norm_gain, offset, part_width, 0)
    input_slab = lax.dynamic_slice_in_dim(widened, offset, part_width, 1)
    scaled = gain_slab[None, :] * part_grad
    inner_sum = jnp.sum(inners, 0).reshape(row_count)
    mean_term = (inner_sum / D)[:, None]
    input_grad = (
        inverse_rms[:, None] * scaled
        - input_slab * (inverse_rms * inverse_rms * inverse_rms)[:, None] * mean_term
    )
    return (
        clipped[:, :width_q],
        clipped[:, width_q : width_q + width_k],
        clipped[:, width_q + width_k :],
        input_grad.astype(jnp.bfloat16)[None],
    )


def solution(mesh):
    return jax.shard_map(
        local,
        mesh=mesh,
        in_specs=(
            P("dp", "seq", None),
            P(("seq", "dp"), "tensor"),
            P(("seq", "dp"), "tensor"),
            P(("seq", "dp"), "tensor"),
            P(),
            P("dp", "seq", "tensor"),
        ),
        out_specs=(
            P(("seq", "dp"), "tensor"),
            P(("seq", "dp"), "tensor"),
            P(("seq", "dp"), "tensor"),
            P("dp", "seq", "tensor"),
        ),
        check_vma=False,
    )
```

```python
import functools
import math

import jax
import jax.numpy as jnp
from jax import lax
from jax.experimental import pallas as pl
from jax.experimental.pallas import tpu as pltpu
from jax.sharding import PartitionSpec as P

D = 3584
H = 8
KVH = 4
HD = 256
WINDOW = 256


EPSILON = 1e-06
SOFTCAP = 50.0
CLIP_BOUND = 1.0
ROPE_BASE = 10000.0


def shifted(value, axis, steps):
    count = lax.axis_size(axis)
    leading, last = (max(0, -steps), min(count, count - steps))
    return lax.ppermute(value, axis, [(source, source + steps) for source in range(leading, last)])


def angles(positions, head_width):
    frequency = ROPE_BASE ** (-2.0 * jnp.arange(head_width // 2).astype(jnp.float32) / head_width)
    phases = positions.astype(jnp.float32)[:, None] * frequency[None, :]
    return (jnp.cos(phases)[:, None, :], jnp.sin(phases)[:, None, :])


def rotate(vectors, cosine, sine_part, direction):
    half_width = vectors.shape[-1] // 2
    first_half = vectors[..., :half_width]
    second_half = vectors[..., half_width:]
    return jnp.concatenate(
        [
            first_half * cosine - direction * second_half * sine_part,
            second_half * cosine + direction * first_half * sine_part,
        ],
        -1,
    )


def attend(queries, key_rows, value_rows, query_pos, key_pos, cotangent):
    query_count, head_count, head_width = queries.shape
    kv_heads = key_rows.shape[1]
    group_size = head_count // kv_heads
    grouped_query = queries.reshape(query_count, kv_heads, group_size, head_width)
    grouped_cot = cotangent.reshape(query_count, kv_heads, group_size, head_width)
    inv_scale = 1.0 / math.sqrt(head_width)
    logits = (
        jnp.einsum("tkgd,skd->kgts", grouped_query, key_rows, preferred_element_type=jnp.float32)
        * inv_scale
    )
    squash = jnp.tanh(logits / SOFTCAP)
    allowed = (
        (key_pos[None, :] <= query_pos[:, None])
        & (key_pos[None, :] > query_pos[:, None] - WINDOW)
        & (key_pos[None, :] >= 0)
    )
    exp_terms = jnp.where(allowed, jnp.exp(SOFTCAP * squash), 0.0)
    softmax = exp_terms / jnp.sum(exp_terms, -1, keepdims=True)
    probs_low = softmax.astype(jnp.bfloat16)
    dsoftmax = jnp.einsum(
        "tkgd,skd->kgts", grouped_cot, value_rows, preferred_element_type=jnp.float32
    )
    value_grads = jnp.einsum(
        "kgts,tkgd->skd", probs_low, grouped_cot, preferred_element_type=jnp.float32
    )
    row_delta = jnp.sum(softmax * dsoftmax, -1, keepdims=True)
    dlogits = (softmax * (dsoftmax - row_delta) * (1.0 - squash * squash) * inv_scale).astype(
        jnp.bfloat16
    )
    dquery = jnp.einsum("kgts,skd->tkgd", dlogits, key_rows, preferred_element_type=jnp.float32)
    key_grads = jnp.einsum(
        "kgts,tkgd->skd", dlogits, grouped_query, preferred_element_type=jnp.float32
    )
    return (dquery.reshape(query_count, head_count, head_width), key_grads, value_grads)


MESH = pl.DeviceIdType.MESH


def greet(axes, peers=()):
    barrier = pltpu.get_barrier_semaphore()
    for axis in axes:
        count = lax.axis_size(axis)
        me = lax.axis_index(axis)
        for step in (1, -1):

            @pl.when((me + step >= 0) & (me + step < count))
            def _():
                pl.semaphore_signal(
                    barrier, inc=1, device_id={axis: me + step}, device_id_type=MESH
                )

    for peer in peers:
        pl.semaphore_signal(barrier, inc=1, device_id=peer, device_id_type=MESH)
    near = len(peers)
    for axis in axes:
        me = lax.axis_index(axis)
        near = near + jnp.minimum(me, 1) + jnp.minimum(lax.axis_size(axis) - 1 - me, 1)
    pl.semaphore_wait(barrier, near)


class LineGather:
    def __init__(self, order, part, first, second, low, high, x_ref, out_ref, send_sem, recv_sem):
        self.order = order
        self.part, self.first, self.second = part, first, second
        self.rows = pl.ds(low, high - low)
        self.x_ref, self.out_ref = x_ref, out_ref
        self.send_sem, self.recv_sem = send_sem, recv_sem
        self.me = {axis: lax.axis_index(axis) for axis in (first, second)}
        self.count = {axis: lax.axis_size(axis) for axis in (first, second)}
        self.sends = []

    def slot(self, at):
        return self.out_ref.at[tuple(at[axis] for axis in self.order) + (self.rows,)]

    def copy(self, at, axis, step, own):
        way = (0 if axis == "seq" else 2) + (0 if step == 1 else 1)
        return pltpu.make_async_remote_copy(
            src_ref=self.x_ref.at[self.rows] if own else self.slot(at),
            dst_ref=self.slot(at),
            send_sem=self.send_sem.at[self.part, way, at["seq"], at["dp"]],
            recv_sem=self.recv_sem.at[self.part, at["seq"], at["dp"]],
            device_id={axis: self.me[axis] + step},
            device_id_type=MESH,
        )

    def inside(self, axis, value):
        return (value >= 0) & (value < self.count[axis])

    def send(self, at, axis, step, held, own=False):
        ok = held & self.inside(axis, self.me[axis] + step)

        @pl.when(ok)
        def _():
            self.copy(at, axis, step, own).start()

        self.sends.append((at, axis, step, ok, own))

    def receive(self, at, held):
        @pl.when(held)
        def _():
            self.copy(at, self.first, 1, False).wait_recv()

    def steps(self):
        first, second = self.first, self.second
        here = jnp.bool_(True)
        for axis in (first, second):
            for step in (1, -1):
                self.send(dict(self.me), axis, step, here, True)
        yield
        column = [(dict(self.me), here, True)]
        for hop in range(1, self.count[first]):
            for step in (1, -1):
                at = {**self.me, first: self.me[first] - step * hop}
                held = self.inside(first, at[first])
                self.receive(at, held)
                self.send(at, first, step, held)
                for way in (1, -1):
                    self.send(at, second, way, held)
                column.append((at, held, False))
            yield
        for hop in range(1, self.count[second]):
            for base, held_base, _ in column:
                for step in (1, -1):
                    at = {**base, second: self.me[second] - step * hop}
                    held = held_base & self.inside(second, at[second])
                    self.receive(at, held)
                    self.send(at, second, step, held)
            yield

    def finish(self):
        for at, axis, step, ok, own in self.sends:

            @pl.when(ok)
            def _():
                self.copy(at, axis, step, own).wait_send()


def run_gathers(gathers):
    live = [gather.steps() for gather in gathers]
    while live:
        still = []
        for walk in live:
            try:
                next(walk)
                still.append(walk)
            except StopIteration:
                pass
        live = still
    for gather in gathers:
        gather.finish()


def head_kernel(
    cut, x_ref, block_ref, out_ref, blocks_ref, send_sem, recv_sem, own_sem, *exchange_sems
):
    rows = x_ref.shape[0]
    seq, dp = lax.axis_index("seq"), lax.axis_index("dp")
    owns = [
        pltpu.make_async_copy(x_ref, out_ref.at[seq, dp], own_sem.at[0]),
        pltpu.make_async_copy(block_ref.at[seq, dp], blocks_ref.at[dp, seq], own_sem.at[1]),
    ]
    for own in owns:
        own.start()
    _, peers = block_peers()
    greet(
        (),
        [{"seq": seq, "dp": dp} for _, seq, dp in peers]
        + [{"tensor": other} for other in tensor_peers()],
    )
    order = ("seq", "dp")
    run_gathers(
        [
            LineGather(order, 0, "seq", "dp", 0, cut, x_ref, out_ref, send_sem, recv_sem),
            LineGather(order, 1, "dp", "seq", cut, rows, x_ref, out_ref, send_sem, recv_sem),
            Exchange(block_ref, blocks_ref, *exchange_sems),
        ]
    )
    for own in owns:
        own.wait()


def gather_and_exchange(x, blocks, cut, collective_id):
    shape = (lax.axis_size("seq"), lax.axis_size("dp"))
    return pl.pallas_call(
        functools.partial(head_kernel, cut),
        out_shape=(
            jax.ShapeDtypeStruct(shape + x.shape, x.dtype),
            jax.ShapeDtypeStruct((shape[1], shape[0]) + blocks.shape[2:], blocks.dtype),
        ),
        in_specs=[pl.BlockSpec(memory_space=pltpu.VMEM)] * 2,
        out_specs=(pl.BlockSpec(memory_space=pl.ANY),) * 2,
        scratch_shapes=[
            pltpu.SemaphoreType.DMA((2, 4) + shape),
            pltpu.SemaphoreType.DMA((2,) + shape),
            pltpu.SemaphoreType.DMA((2,)),
        ]
        + exchange_semaphores(),
        compiler_params=pltpu.CompilerParams(
            collective_id=collective_id, has_side_effects=True
        ),
    )(x, blocks)


def tail_kernel(
    cut,
    order,
    x_ref,
    part_ref,
    inner_ref,
    out_ref,
    parts_ref,
    inners_ref,
    send_sem,
    recv_sem,
    own_sem,
    part_send,
    part_recv,
    inner_send,
    inner_recv,
):
    rows = x_ref.shape[0]
    count, me = lax.axis_size("tensor"), lax.axis_index("tensor")
    width = part_ref.shape[1] // count

    def slab(index):
        return part_ref.at[:, pl.ds(pl.multiple_of(index * width, 128), width)]

    owns = [
        pltpu.make_async_copy(
            x_ref, out_ref.at[tuple(lax.axis_index(axis) for axis in order)], own_sem.at[0]
        ),
        pltpu.make_async_copy(slab(me), parts_ref.at[me], own_sem.at[1]),
        pltpu.make_async_copy(inner_ref, inners_ref.at[me], own_sem.at[2]),
    ]
    for own in owns:
        own.start()
    others = [lax.rem(me + hop, count) for hop in range(1, count)]
    greet(("seq", "dp"), [{"tensor": other} for other in others])
    copies = []
    for index, other in enumerate(others):
        copies.append(
            pltpu.make_async_remote_copy(
                src_ref=slab(other),
                dst_ref=parts_ref.at[me],
                send_sem=part_send.at[index],
                recv_sem=part_recv.at[index],
                device_id={"tensor": other},
                device_id_type=MESH,
            )
        )
        copies.append(
            pltpu.make_async_remote_copy(
                src_ref=inner_ref,
                dst_ref=inners_ref.at[me],
                send_sem=inner_send.at[index],
                recv_sem=inner_recv.at[index],
                device_id={"tensor": other},
                device_id_type=MESH,
            )
        )
    for copy in copies:
        copy.start()
    run_gathers(
        [
            LineGather(order, 0, "seq", "dp", 0, cut, x_ref, out_ref, send_sem, recv_sem),
            LineGather(order, 1, "dp", "seq", cut, rows, x_ref, out_ref, send_sem, recv_sem),
        ]
    )
    for copy in copies:
        copy.wait()
    for own in owns:
        own.wait()


def gather_and_scatter(x, part, inner, cut, order, collective_id):
    shape = (lax.axis_size("seq"), lax.axis_size("dp"))
    count = lax.axis_size("tensor")
    return pl.pallas_call(
        functools.partial(tail_kernel, cut, order),
        out_shape=(
            jax.ShapeDtypeStruct(tuple(lax.axis_size(axis) for axis in order) + x.shape, x.dtype),
            jax.ShapeDtypeStruct((count, part.shape[0], part.shape[1] // count), part.dtype),
            jax.ShapeDtypeStruct((count,) + inner.shape, inner.dtype),
        ),
        in_specs=[pl.BlockSpec(memory_space=pltpu.VMEM)] * 3,
        out_specs=(pl.BlockSpec(memory_space=pl.ANY),) * 3,
        scratch_shapes=[
            pltpu.SemaphoreType.DMA((2, 4) + shape),
            pltpu.SemaphoreType.DMA((2,) + shape),
            pltpu.SemaphoreType.DMA((3,)),
        ]
        + [pltpu.SemaphoreType.DMA((count - 1,))] * 4,
        compiler_params=pltpu.CompilerParams(
            collective_id=collective_id, has_side_effects=True
        ),
    )(x, part, inner)


def block_peers():
    seqs, dps = lax.axis_size("seq"), lax.axis_size("dp")
    mine = lax.axis_index("dp") * seqs + lax.axis_index("seq")
    others = [lax.rem(mine + hop, seqs * dps) for hop in range(1, seqs * dps)]
    return mine, [(other, lax.rem(other, seqs), other // seqs) for other in others]


def tensor_peers():
    count, me = lax.axis_size("tensor"), lax.axis_index("tensor")
    return [lax.rem(me + hop, count) for hop in range(1, count)]


class Exchange:
    def __init__(self, x_ref, out_ref, send_sem, recv_sem, pass_sem):
        self.x_ref, self.out_ref = x_ref, out_ref
        self.send_sem, self.recv_sem, self.pass_sem = send_sem, recv_sem, pass_sem
        self.seqs, self.dps = lax.axis_size("seq"), lax.axis_size("dp")
        self.lanes, self.lane = lax.axis_size("tensor"), lax.axis_index("tensor")
        self.mine, self.peers = block_peers()
        self.sender = lax.rem(self.mine, self.lanes) == self.lane

    def slot(self, index):
        return self.out_ref.at[index // self.seqs, lax.rem(index, self.seqs)]

    def first(self, hop):
        _, seq, dp = self.peers[hop]
        return pltpu.make_async_remote_copy(
            src_ref=self.x_ref.at[seq, dp],
            dst_ref=self.slot(self.mine),
            send_sem=self.send_sem.at[hop],
            recv_sem=self.recv_sem.at[self.mine],
            device_id={"seq": seq, "dp": dp},
            device_id_type=MESH,
        )

    def onward(self, index, step, hop, other):
        return pltpu.make_async_remote_copy(
            src_ref=self.slot(index),
            dst_ref=self.slot(index),
            send_sem=self.pass_sem.at[step, hop],
            recv_sem=self.recv_sem.at[index],
            device_id={"tensor": other},
            device_id_type=MESH,
        )

    def owned(self, lane):
        return [lane + step * self.lanes for step in range(self.seqs * self.dps // self.lanes)]

    def steps(self):
        @pl.when(self.sender)
        def _():
            for hop in range(len(self.peers)):
                self.first(hop).start()

        yield
        others = tensor_peers()
        for step, index in enumerate(self.owned(self.lane)):

            @pl.when(index != self.mine)
            def _():
                self.onward(index, step, 0, others[0]).wait_recv()
                for hop, other in enumerate(others):
                    self.onward(index, step, hop, other).start()

        yield

    def finish(self):
        others = tensor_peers()
        for other in others:
            for index in self.owned(other):

                @pl.when(index != self.mine)
                def _():
                    self.onward(index, 0, 0, other).wait_recv()

        for step, index in enumerate(self.owned(self.lane)):

            @pl.when(index != self.mine)
            def _():
                for hop, other in enumerate(others):
                    self.onward(index, step, hop, other).wait_send()

        @pl.when(self.sender)
        def _():
            for hop in range(len(self.peers)):
                self.first(hop).wait_send()


def exchange_semaphores():
    count, lanes = lax.axis_size("seq") * lax.axis_size("dp"), lax.axis_size("tensor")
    return [
        pltpu.SemaphoreType.DMA((count - 1,)),
        pltpu.SemaphoreType.DMA((count,)),
        pltpu.SemaphoreType.DMA((count // lanes, lanes - 1)),
    ]


def total_kernel(x_ref, out_ref, held, send_sem, recv_sem, send_wide, recv_wide, own_sem):
    mine, peers = block_peers()
    lane = lax.axis_index("tensor")
    others = tensor_peers()
    own = pltpu.make_async_copy(x_ref, held.at[lane, mine], own_sem)
    own.start()
    greet(
        (),
        [{"seq": seq, "dp": dp} for _, seq, dp in peers] + [{"tensor": other} for other in others],
    )
    near = [
        pltpu.make_async_remote_copy(
            src_ref=x_ref,
            dst_ref=held.at[lane, mine],
            send_sem=send_sem.at[hop],
            recv_sem=recv_sem.at[mine],
            device_id={"seq": seq, "dp": dp},
            device_id_type=MESH,
        )
        for hop, (_, seq, dp) in enumerate(peers)
    ]
    for copy in near:
        copy.start()
    for index, seq, dp in peers:
        pltpu.make_async_remote_copy(
            src_ref=x_ref,
            dst_ref=held.at[lane, index],
            send_sem=send_sem.at[0],
            recv_sem=recv_sem.at[index],
            device_id={"seq": seq, "dp": dp},
            device_id_type=MESH,
        ).wait_recv()
    own.wait()
    far = [
        pltpu.make_async_remote_copy(
            src_ref=held.at[lane],
            dst_ref=held.at[lane],
            send_sem=send_wide.at[hop],
            recv_sem=recv_wide.at[hop],
            device_id={"tensor": other},
            device_id_type=MESH,
        )
        for hop, other in enumerate(others)
    ]
    for copy in far:
        copy.start()
    for copy in far:
        copy.wait()
    for copy in near:
        copy.wait_send()
    out_ref[...] = jnp.sum(held[...], (0, 1))


def total_of(x, collective_id):
    count, lanes = lax.axis_size("seq") * lax.axis_size("dp"), lax.axis_size("tensor")
    return pl.pallas_call(
        total_kernel,
        out_shape=jax.ShapeDtypeStruct(x.shape, x.dtype),
        in_specs=[pl.BlockSpec(memory_space=pltpu.VMEM)],
        out_specs=pl.BlockSpec(memory_space=pltpu.VMEM),
        scratch_shapes=[
            pltpu.VMEM((lanes, count) + x.shape, x.dtype),
            pltpu.SemaphoreType.DMA((count - 1,)),
            pltpu.SemaphoreType.DMA((count,)),
            pltpu.SemaphoreType.DMA((lanes - 1,)),
            pltpu.SemaphoreType.DMA((lanes - 1,)),
            pltpu.SemaphoreType.DMA,
        ],
        compiler_params=pltpu.CompilerParams(
            collective_id=collective_id, has_side_effects=True
        ),
    )(x)


def cut_of(rows):
    return max(16, rows // 7 // 16 * 16)


def local(inputs, w_query, w_key, w_value, norm_gain, attn_grad):
    widened = inputs[0].astype(jnp.float32)
    row_count = widened.shape[0]
    inverse_rms = lax.rsqrt(jnp.mean(widened * widened, -1) + EPSILON)
    normed = (widened * inverse_rms[:, None] * norm_gain[None, :]).astype(jnp.bfloat16)
    width_q = w_query.shape[1]
    width_k = w_key.shape[1]
    local_w = jnp.concatenate([w_query, w_key, w_value], 1)
    seqs, dps = lax.axis_size("seq"), lax.axis_size("dp")
    rows_w = local_w.shape[0]
    full_w, slabs = gather_and_exchange(
        local_w, normed.T.reshape(seqs, dps, rows_w, row_count), cut_of(rows_w), 0
    )
    full_w = full_w.reshape(seqs * dps * rows_w, -1)
    projected = jnp.dot(normed, full_w, preferred_element_type=jnp.float32)
    start_row = lax.axis_index("seq") * row_count
    query_pos = start_row + jnp.arange(row_count, dtype=jnp.int32)
    key_pos = start_row - row_count + jnp.arange(2 * row_count, dtype=jnp.int32)
    cosine, sine_part = angles(query_pos, HD)
    heads_q = width_q // HD
    heads_k = width_k // HD
    rotated_query = rotate(
        projected[:, :width_q].reshape(row_count, heads_q, HD), cosine, sine_part, 1.0
    ).astype(jnp.bfloat16)
    rotated_keys = rotate(
        projected[:, width_q : width_q + width_k].reshape(row_count, heads_k, HD),
        cosine,
        sine_part,
        1.0,
    ).astype(jnp.bfloat16)
    value_rows = (
        projected[:, width_q + width_k :].reshape(row_count, heads_k, HD).astype(jnp.bfloat16)
    )
    keys_before, values_before = shifted((rotated_keys, value_rows), "seq", 1)
    dquery, key_ext_grad, value_ext_grad = attend(
        rotated_query,
        jnp.concatenate([keys_before, rotated_keys], 0),
        jnp.concatenate([values_before, value_rows], 0),
        query_pos,
        key_pos,
        attn_grad[0],
    )
    back_keys, back_values = shifted(
        (key_ext_grad[:row_count], value_ext_grad[:row_count]), "seq", -1
    )
    key_grads = key_ext_grad[row_count:] + back_keys
    value_grads = value_ext_grad[row_count:] + back_values
    dquery = rotate(dquery, cosine, sine_part, -1.0)
    key_grads = rotate(key_grads, cosine, sine_part, -1.0)
    d_out = jnp.concatenate(
        [
            dquery.reshape(row_count, width_q),
            key_grads.reshape(row_count, width_k),
            value_grads.reshape(row_count, width_k),
        ],
        1,
    ).astype(jnp.bfloat16)
    dnormed = lax.dot_general(
        d_out, full_w, (((1,), (1,)), ((), ())), preferred_element_type=jnp.float32
    )
    inner = jnp.sum(widened * norm_gain[None, :] * dnormed, -1).reshape(-1, 128)
    cotangents, parts, inners = gather_and_scatter(
        d_out, dnormed.astype(jnp.bfloat16), inner, cut_of(row_count), ("dp", "seq"), 2
    )
    grads = []
    for example in range(dps):
        grads.append(
            sum(
                jnp.dot(
                    slabs[example, s], cotangents[example, s], preferred_element_type=jnp.float32
                )
                for s in range(seqs)
            )
        )
    squares = jnp.stack([jnp.sum(grad * grad) for grad in grads])
    square_sum = total_of(jnp.broadcast_to(squares[:, None], (dps, 128)), 1)[:, 0]
    grad_rms = jnp.sqrt(square_sum / (D * (H + 2 * KVH) * HD) + EPSILON)
    factor = CLIP_BOUND / jnp.maximum(grad_rms, CLIP_BOUND)
    clipped = sum(factor[example] * grads[example] for example in range(dps))
    part_width = D // lax.axis_size("tensor")
    offset = lax.axis_index("tensor") * part_width
    part_grad = jnp.sum(parts.astype(jnp.float32), 0)
    gain_slab = lax.dynamic_slice_in_dim(norm_gain, offset, part_width, 0)
    input_slab = lax.dynamic_slice_in_dim(widened, offset, part_width, 1)
    scaled = gain_slab[None, :] * part_grad
    inner_sum = jnp.sum(inners, 0).reshape(row_count)
    mean_term = (inner_sum / D)[:, None]
    input_grad = (
        inverse_rms[:, None] * scaled
        - input_slab * (inverse_rms * inverse_rms * inverse_rms)[:, None] * mean_term
    )
    return (
        clipped[:, :width_q],
        clipped[:, width_q : width_q + width_k],
        clipped[:, width_q + width_k :],
        input_grad.astype(jnp.bfloat16)[None],
    )


def solution(mesh):
    return jax.shard_map(
        local,
        mesh=mesh,
        in_specs=(
            P("dp", "seq", None),
            P(("seq", "dp"), "tensor"),
            P(("seq", "dp"), "tensor"),
            P(("seq", "dp"), "tensor"),
            P(),
            P("dp", "seq", "tensor"),
        ),
        out_specs=(
            P(("seq", "dp"), "tensor"),
            P(("seq", "dp"), "tensor"),
            P(("seq", "dp"), "tensor"),
            P("dp", "seq", "tensor"),
        ),
        check_vma=False,
    )
```

```python
import functools
import math

import jax
import jax.numpy as jnp
from jax import lax
from jax.experimental import pallas as pl
from jax.experimental.pallas import tpu as pltpu
from jax.sharding import PartitionSpec as P

D = 3584
H = 8
KVH = 4
HD = 256
WINDOW = 256


EPSILON = 1e-06
SOFTCAP = 50.0
CLIP_BOUND = 1.0
ROPE_BASE = 10000.0


def angles(positions, head_width):
    frequency = ROPE_BASE ** (-2.0 * jnp.arange(head_width // 2).astype(jnp.float32) / head_width)
    phases = positions.astype(jnp.float32)[:, None] * frequency[None, :]
    return (jnp.cos(phases)[:, None, :], jnp.sin(phases)[:, None, :])


MESH = pl.DeviceIdType.MESH


def greet(axes, peers=()):
    barrier = pltpu.get_barrier_semaphore()
    for axis in axes:
        count = lax.axis_size(axis)
        me = lax.axis_index(axis)
        for step in (1, -1):

            @pl.when((me + step >= 0) & (me + step < count))
            def _():
                pl.semaphore_signal(
                    barrier, inc=1, device_id={axis: me + step}, device_id_type=MESH
                )

    for peer in peers:
        pl.semaphore_signal(barrier, inc=1, device_id=peer, device_id_type=MESH)
    near = len(peers)
    for axis in axes:
        me = lax.axis_index(axis)
        near = near + jnp.minimum(me, 1) + jnp.minimum(lax.axis_size(axis) - 1 - me, 1)
    pl.semaphore_wait(barrier, near)


class LineGather:
    def __init__(self, order, part, first, second, low, high, x_ref, out_ref, send_sem, recv_sem):
        self.order = order
        self.part, self.first, self.second = part, first, second
        self.rows = pl.ds(low, high - low)
        self.x_ref, self.out_ref = x_ref, out_ref
        self.send_sem, self.recv_sem = send_sem, recv_sem
        self.me = {axis: lax.axis_index(axis) for axis in (first, second)}
        self.count = {axis: lax.axis_size(axis) for axis in (first, second)}
        self.sends = []

    def slot(self, at):
        return self.out_ref.at[tuple(at[axis] for axis in self.order) + (self.rows,)]

    def copy(self, at, axis, step, own):
        way = (0 if axis == "seq" else 2) + (0 if step == 1 else 1)
        return pltpu.make_async_remote_copy(
            src_ref=self.x_ref.at[self.rows] if own else self.slot(at),
            dst_ref=self.slot(at),
            send_sem=self.send_sem.at[self.part, way, at["seq"], at["dp"]],
            recv_sem=self.recv_sem.at[self.part, at["seq"], at["dp"]],
            device_id={axis: self.me[axis] + step},
            device_id_type=MESH,
        )

    def inside(self, axis, value):
        return (value >= 0) & (value < self.count[axis])

    def send(self, at, axis, step, held, own=False):
        ok = held & self.inside(axis, self.me[axis] + step)

        @pl.when(ok)
        def _():
            self.copy(at, axis, step, own).start()

        self.sends.append((at, axis, step, ok, own))

    def receive(self, at, held):
        @pl.when(held)
        def _():
            self.copy(at, self.first, 1, False).wait_recv()

    def steps(self):
        first, second = self.first, self.second
        here = jnp.bool_(True)
        for axis in (first, second):
            for step in (1, -1):
                self.send(dict(self.me), axis, step, here, True)
        yield
        column = [(dict(self.me), here, True)]
        for hop in range(1, self.count[first]):
            for step in (1, -1):
                at = {**self.me, first: self.me[first] - step * hop}
                held = self.inside(first, at[first])
                self.receive(at, held)
                self.send(at, first, step, held)
                for way in (1, -1):
                    self.send(at, second, way, held)
                column.append((at, held, False))
            yield
        for hop in range(1, self.count[second]):
            for base, held_base, _ in column:
                for step in (1, -1):
                    at = {**base, second: self.me[second] - step * hop}
                    held = held_base & self.inside(second, at[second])
                    self.receive(at, held)
                    self.send(at, second, step, held)
            yield

    def finish(self):
        for at, axis, step, ok, own in self.sends:

            @pl.when(ok)
            def _():
                self.copy(at, axis, step, own).wait_send()


def run_gathers(gathers):
    live = [gather.steps() for gather in gathers]
    while live:
        still = []
        for walk in live:
            try:
                next(walk)
                still.append(walk)
            except StopIteration:
                pass
        live = still
    for gather in gathers:
        gather.finish()


def gather_kernel(cut, order, x_ref, out_ref, send_sem, recv_sem, own_sem):
    rows = x_ref.shape[0]
    own = pltpu.make_async_copy(
        x_ref, out_ref.at[tuple(lax.axis_index(axis) for axis in order)], own_sem
    )
    own.start()
    greet(("seq", "dp"))
    run_gathers(
        [
            LineGather(order, 0, "seq", "dp", 0, cut, x_ref, out_ref, send_sem, recv_sem),
            LineGather(order, 1, "dp", "seq", cut, rows, x_ref, out_ref, send_sem, recv_sem),
        ]
    )
    own.wait()


def gather_blocks(x, cut, order, collective_id):
    shape = (lax.axis_size("seq"), lax.axis_size("dp"))
    return pl.pallas_call(
        functools.partial(gather_kernel, cut, order),
        out_shape=jax.ShapeDtypeStruct(
            tuple(lax.axis_size(axis) for axis in order) + x.shape, x.dtype
        ),
        in_specs=[pl.BlockSpec(memory_space=pltpu.VMEM)],
        out_specs=pl.BlockSpec(memory_space=pl.ANY),
        scratch_shapes=[
            pltpu.SemaphoreType.DMA((2, 4) + shape),
            pltpu.SemaphoreType.DMA((2,) + shape),
            pltpu.SemaphoreType.DMA,
        ],
        compiler_params=pltpu.CompilerParams(
            collective_id=collective_id, has_side_effects=True
        ),
    )(x)


def tail_kernel(
    cut,
    order,
    x_ref,
    part_ref,
    inner_ref,
    out_ref,
    parts_ref,
    inners_ref,
    send_sem,
    recv_sem,
    own_sem,
    part_send,
    part_recv,
    inner_send,
    inner_recv,
):
    rows = x_ref.shape[0]
    count, me = lax.axis_size("tensor"), lax.axis_index("tensor")
    width = part_ref.shape[1] // count

    def slab(index):
        return part_ref.at[:, pl.ds(pl.multiple_of(index * width, 128), width)]

    owns = [
        pltpu.make_async_copy(
            x_ref, out_ref.at[tuple(lax.axis_index(axis) for axis in order)], own_sem.at[0]
        ),
        pltpu.make_async_copy(slab(me), parts_ref.at[me], own_sem.at[1]),
        pltpu.make_async_copy(inner_ref, inners_ref.at[me], own_sem.at[2]),
    ]
    for own in owns:
        own.start()
    others = [lax.rem(me + hop, count) for hop in range(1, count)]
    greet(("seq", "dp"), [{"tensor": other} for other in others])
    copies = []
    for index, other in enumerate(others):
        copies.append(
            pltpu.make_async_remote_copy(
                src_ref=slab(other),
                dst_ref=parts_ref.at[me],
                send_sem=part_send.at[index],
                recv_sem=part_recv.at[index],
                device_id={"tensor": other},
                device_id_type=MESH,
            )
        )
        copies.append(
            pltpu.make_async_remote_copy(
                src_ref=inner_ref,
                dst_ref=inners_ref.at[me],
                send_sem=inner_send.at[index],
                recv_sem=inner_recv.at[index],
                device_id={"tensor": other},
                device_id_type=MESH,
            )
        )
    for copy in copies:
        copy.start()
    run_gathers(
        [
            LineGather(order, 0, "seq", "dp", 0, cut, x_ref, out_ref, send_sem, recv_sem),
            LineGather(order, 1, "dp", "seq", cut, rows, x_ref, out_ref, send_sem, recv_sem),
        ]
    )
    for copy in copies:
        copy.wait()
    for own in owns:
        own.wait()


def gather_and_scatter(x, part, inner, cut, order, collective_id):
    shape = (lax.axis_size("seq"), lax.axis_size("dp"))
    count = lax.axis_size("tensor")
    return pl.pallas_call(
        functools.partial(tail_kernel, cut, order),
        out_shape=(
            jax.ShapeDtypeStruct(tuple(lax.axis_size(axis) for axis in order) + x.shape, x.dtype),
            jax.ShapeDtypeStruct((count, part.shape[0], part.shape[1] // count), part.dtype),
            jax.ShapeDtypeStruct((count,) + inner.shape, inner.dtype),
        ),
        in_specs=[pl.BlockSpec(memory_space=pltpu.VMEM)] * 3,
        out_specs=(pl.BlockSpec(memory_space=pl.ANY),) * 3,
        scratch_shapes=[
            pltpu.SemaphoreType.DMA((2, 4) + shape),
            pltpu.SemaphoreType.DMA((2,) + shape),
            pltpu.SemaphoreType.DMA((3,)),
        ]
        + [pltpu.SemaphoreType.DMA((count - 1,))] * 4,
        compiler_params=pltpu.CompilerParams(
            collective_id=collective_id, has_side_effects=True
        ),
    )(x, part, inner)


def block_peers():
    seqs, dps = lax.axis_size("seq"), lax.axis_size("dp")
    mine = lax.axis_index("dp") * seqs + lax.axis_index("seq")
    others = [lax.rem(mine + hop, seqs * dps) for hop in range(1, seqs * dps)]
    return mine, [(other, lax.rem(other, seqs), other // seqs) for other in others]


def tensor_peers():
    count, me = lax.axis_size("tensor"), lax.axis_index("tensor")
    return [lax.rem(me + hop, count) for hop in range(1, count)]


class Exchange:
    def __init__(self, x_ref, out_ref, send_sem, recv_sem, pass_sem):
        self.x_ref, self.out_ref = x_ref, out_ref
        self.send_sem, self.recv_sem, self.pass_sem = send_sem, recv_sem, pass_sem
        self.seqs, self.dps = lax.axis_size("seq"), lax.axis_size("dp")
        self.lanes, self.lane = lax.axis_size("tensor"), lax.axis_index("tensor")
        self.mine, self.peers = block_peers()
        self.sender = lax.rem(self.mine, self.lanes) == self.lane

    def slot(self, index):
        return self.out_ref.at[index // self.seqs, lax.rem(index, self.seqs)]

    def first(self, hop):
        _, seq, dp = self.peers[hop]
        return pltpu.make_async_remote_copy(
            src_ref=self.x_ref.at[seq, dp],
            dst_ref=self.slot(self.mine),
            send_sem=self.send_sem.at[hop],
            recv_sem=self.recv_sem.at[self.mine],
            device_id={"seq": seq, "dp": dp},
            device_id_type=MESH,
        )

    def onward(self, index, step, hop, other):
        return pltpu.make_async_remote_copy(
            src_ref=self.slot(index),
            dst_ref=self.slot(index),
            send_sem=self.pass_sem.at[step, hop],
            recv_sem=self.recv_sem.at[index],
            device_id={"tensor": other},
            device_id_type=MESH,
        )

    def owned(self, lane):
        return [lane + step * self.lanes for step in range(self.seqs * self.dps // self.lanes)]

    def steps(self):
        @pl.when(self.sender)
        def _():
            for hop in range(len(self.peers)):
                self.first(hop).start()

        yield
        others = tensor_peers()
        for step, index in enumerate(self.owned(self.lane)):

            @pl.when(index != self.mine)
            def _():
                self.onward(index, step, 0, others[0]).wait_recv()
                for hop, other in enumerate(others):
                    self.onward(index, step, hop, other).start()

        yield

    def finish(self):
        others = tensor_peers()
        for other in others:
            for index in self.owned(other):

                @pl.when(index != self.mine)
                def _():
                    self.onward(index, 0, 0, other).wait_recv()

        for step, index in enumerate(self.owned(self.lane)):

            @pl.when(index != self.mine)
            def _():
                for hop, other in enumerate(others):
                    self.onward(index, step, hop, other).wait_send()

        @pl.when(self.sender)
        def _():
            for hop in range(len(self.peers)):
                self.first(hop).wait_send()


def exchange_semaphores():
    count, lanes = lax.axis_size("seq") * lax.axis_size("dp"), lax.axis_size("tensor")
    return [
        pltpu.SemaphoreType.DMA((count - 1,)),
        pltpu.SemaphoreType.DMA((count,)),
        pltpu.SemaphoreType.DMA((count // lanes, lanes - 1)),
    ]


def turn(vectors, cosine, sine_part, direction):
    half = vectors.shape[-1] // 2
    low, high = vectors[:, :half], vectors[:, half:]
    return jnp.concatenate(
        [
            low * cosine - direction * high * sine_part,
            high * cosine + direction * low * sine_part,
        ],
        -1,
    )


def product(left, right, left_dim, right_dim):
    return lax.dot_general(
        left, right, (((left_dim,), (right_dim,)), ((), ())), preferred_element_type=jnp.float32
    )


def attend_kernel(
    width_q,
    proj_ref,
    cos_ref,
    sin_ref,
    cot_ref,
    block_ref,
    out_ref,
    blocks_ref,
    held,
    before,
    back_out,
    back_in,
    own_grad,
    own_sem,
    kv_sems,
    back_sems,
    *exchange_sems,
):
    rows = proj_ref.shape[0]
    width_k = (proj_ref.shape[1] - width_q) // 2
    heads_k = width_k // HD
    group = width_q // width_k
    inv_scale = 1.0 / math.sqrt(HD)
    seqs, seq, dp = lax.axis_size("seq"), lax.axis_index("seq"), lax.axis_index("dp")
    own = pltpu.make_async_copy(block_ref.at[seq, dp], blocks_ref.at[dp, seq], own_sem)
    own.start()
    cosine, sine_part = cos_ref[...], sin_ref[...]
    for head in range(heads_k):
        low = head * HD
        at = slice(low, low + HD)
        keys = proj_ref[:, width_q + low : width_q + low + HD]
        held[:, at] = turn(keys, cosine, sine_part, 1.0).astype(jnp.bfloat16)
        values = proj_ref[:, width_q + width_k + low : width_q + width_k + low + HD]
        held[:, width_k + low : width_k + low + HD] = values.astype(jnp.bfloat16)
    _, peers = block_peers()
    greet(
        (),
        [{"seq": other, "dp": far} for _, other, far in peers]
        + [{"tensor": other} for other in tensor_peers()],
    )
    ahead = pltpu.make_async_remote_copy(
        src_ref=held,
        dst_ref=before,
        send_sem=kv_sems.at[0],
        recv_sem=kv_sems.at[1],
        device_id={"seq": seq + 1},
        device_id_type=MESH,
    )
    behind = pltpu.make_async_remote_copy(
        src_ref=back_out,
        dst_ref=back_in,
        send_sem=back_sems.at[0],
        recv_sem=back_sems.at[1],
        device_id={"seq": seq - 1},
        device_id_type=MESH,
    )
    has_next, has_last = seq < seqs - 1, seq > 0

    @pl.when(has_next)
    def _():
        ahead.start()

    exchange = Exchange(block_ref, blocks_ref, *exchange_sems)
    walk = exchange.steps()
    next(walk)

    queries = []
    for head in range(heads_k * group):
        part = proj_ref[:, head * HD : (head + 1) * HD]
        queries.append(turn(part, cosine, sine_part, 1.0).astype(jnp.bfloat16))

    @pl.when(has_last)
    def _():
        ahead.wait_recv()

    @pl.when(jnp.logical_not(has_last))
    def _():
        before[...] = jnp.zeros_like(before)

    query_at = lax.broadcasted_iota(jnp.int32, (rows, rows), 0)
    key_at = lax.broadcasted_iota(jnp.int32, (rows, rows), 1)
    masks = (
        (key_at > query_at + (rows - WINDOW)) & (seq * rows - rows + key_at >= 0),
        (key_at <= query_at) & (key_at > query_at - WINDOW),
    )
    for head in range(heads_k):
        at = slice(head * HD, (head + 1) * HD)
        at_value = slice(width_k + head * HD, width_k + (head + 1) * HD)
        sides = (before, held)
        key_grads, value_grads = [0.0, 0.0], [0.0, 0.0]
        for member in range(group):
            index = head * group + member
            query = queries[index]
            cot = cot_ref[:, index * HD : (index + 1) * HD]
            squashes, terms, slopes = [], [], []
            for side, mask in zip(sides, masks):
                squash = jnp.tanh(product(query, side[:, at], 1, 1) * inv_scale / SOFTCAP)
                squashes.append(squash)
                terms.append(jnp.where(mask, jnp.exp(SOFTCAP * squash), 0.0))
                slopes.append(product(cot, side[:, at_value], 1, 1))
            total = sum(jnp.sum(term, -1, keepdims=True) for term in terms)
            probs = [term / total for term in terms]
            delta = sum(
                jnp.sum(prob * slope, -1, keepdims=True) for prob, slope in zip(probs, slopes)
            )
            dquery = 0.0
            for which in range(2):
                prob, squash = probs[which], squashes[which]
                dlogits = (
                    prob * (slopes[which] - delta) * (1.0 - squash * squash) * inv_scale
                ).astype(jnp.bfloat16)
                dquery = dquery + product(dlogits, sides[which][:, at], 1, 0)
                key_grads[which] = key_grads[which] + product(dlogits, query, 0, 0)
                value_grads[which] = value_grads[which] + product(
                    prob.astype(jnp.bfloat16), cot, 0, 0
                )
            out_ref[:, index * HD : (index + 1) * HD] = turn(
                dquery, cosine, sine_part, -1.0
            ).astype(jnp.bfloat16)
        back_out[:, at] = key_grads[0].astype(jnp.bfloat16)
        back_out[:, at_value] = value_grads[0].astype(jnp.bfloat16)
        own_grad[:, at] = key_grads[1]
        own_grad[:, at_value] = value_grads[1]

    @pl.when(has_last)
    def _():
        behind.start()

    next(walk)

    @pl.when(has_next)
    def _():
        behind.wait_recv()
        own_grad[...] += back_in[...].astype(jnp.float32)

    for head in range(heads_k):
        at = slice(head * HD, (head + 1) * HD)
        out_ref[:, width_q + head * HD : width_q + (head + 1) * HD] = turn(
            own_grad[:, at], cosine, sine_part, -1.0
        ).astype(jnp.bfloat16)
    out_ref[:, width_q + width_k :] = own_grad[:, width_k:].astype(jnp.bfloat16)

    @pl.when(has_next)
    def _():
        ahead.wait_send()

    @pl.when(has_last)
    def _():
        behind.wait_send()

    exchange.finish()
    own.wait()


def attend_and_exchange(projected, cosine, sine_part, cotangent, blocks, collective_id):
    rows, width_q = cotangent.shape
    width_k = (projected.shape[1] - width_q) // 2
    return pl.pallas_call(
        functools.partial(attend_kernel, width_q),
        out_shape=(
            jax.ShapeDtypeStruct(projected.shape, jnp.bfloat16),
            jax.ShapeDtypeStruct(
                (blocks.shape[1], blocks.shape[0]) + blocks.shape[2:], blocks.dtype
            ),
        ),
        in_specs=[pl.BlockSpec(memory_space=pltpu.VMEM)] * 5,
        out_specs=(pl.BlockSpec(memory_space=pltpu.VMEM), pl.BlockSpec(memory_space=pl.ANY)),
        scratch_shapes=[
            pltpu.VMEM((rows, 2 * width_k), jnp.bfloat16),
            pltpu.VMEM((rows, 2 * width_k), jnp.bfloat16),
            pltpu.VMEM((rows, 2 * width_k), jnp.bfloat16),
            pltpu.VMEM((rows, 2 * width_k), jnp.bfloat16),
            pltpu.VMEM((rows, 2 * width_k), jnp.float32),
            pltpu.SemaphoreType.DMA,
            pltpu.SemaphoreType.DMA((2,)),
            pltpu.SemaphoreType.DMA((2,)),
        ]
        + exchange_semaphores(),
        compiler_params=pltpu.CompilerParams(
            collective_id=collective_id, has_side_effects=True
        ),
    )(projected, cosine, sine_part, cotangent, blocks)


def total_kernel(x_ref, out_ref, held, send_sem, recv_sem, send_wide, recv_wide, own_sem):
    mine, peers = block_peers()
    lane = lax.axis_index("tensor")
    others = tensor_peers()
    own = pltpu.make_async_copy(x_ref, held.at[lane, mine], own_sem)
    own.start()
    greet(
        (),
        [{"seq": seq, "dp": dp} for _, seq, dp in peers] + [{"tensor": other} for other in others],
    )
    near = [
        pltpu.make_async_remote_copy(
            src_ref=x_ref,
            dst_ref=held.at[lane, mine],
            send_sem=send_sem.at[hop],
            recv_sem=recv_sem.at[mine],
            device_id={"seq": seq, "dp": dp},
            device_id_type=MESH,
        )
        for hop, (_, seq, dp) in enumerate(peers)
    ]
    for copy in near:
        copy.start()
    for index, seq, dp in peers:
        pltpu.make_async_remote_copy(
            src_ref=x_ref,
            dst_ref=held.at[lane, index],
            send_sem=send_sem.at[0],
            recv_sem=recv_sem.at[index],
            device_id={"seq": seq, "dp": dp},
            device_id_type=MESH,
        ).wait_recv()
    own.wait()
    far = [
        pltpu.make_async_remote_copy(
            src_ref=held.at[lane],
            dst_ref=held.at[lane],
            send_sem=send_wide.at[hop],
            recv_sem=recv_wide.at[hop],
            device_id={"tensor": other},
            device_id_type=MESH,
        )
        for hop, other in enumerate(others)
    ]
    for copy in far:
        copy.start()
    for copy in far:
        copy.wait()
    for copy in near:
        copy.wait_send()
    out_ref[...] = jnp.sum(held[...], (0, 1))


def total_of(x, collective_id):
    count, lanes = lax.axis_size("seq") * lax.axis_size("dp"), lax.axis_size("tensor")
    return pl.pallas_call(
        total_kernel,
        out_shape=jax.ShapeDtypeStruct(x.shape, x.dtype),
        in_specs=[pl.BlockSpec(memory_space=pltpu.VMEM)],
        out_specs=pl.BlockSpec(memory_space=pltpu.VMEM),
        scratch_shapes=[
            pltpu.VMEM((lanes, count) + x.shape, x.dtype),
            pltpu.SemaphoreType.DMA((count - 1,)),
            pltpu.SemaphoreType.DMA((count,)),
            pltpu.SemaphoreType.DMA((lanes - 1,)),
            pltpu.SemaphoreType.DMA((lanes - 1,)),
            pltpu.SemaphoreType.DMA,
        ],
        compiler_params=pltpu.CompilerParams(
            collective_id=collective_id, has_side_effects=True
        ),
    )(x)


def cut_of(rows):
    return max(16, rows // 7 // 16 * 16)


def local(inputs, w_query, w_key, w_value, norm_gain, attn_grad):
    widened = inputs[0].astype(jnp.float32)
    row_count = widened.shape[0]
    inverse_rms = lax.rsqrt(jnp.mean(widened * widened, -1) + EPSILON)
    normed = (widened * inverse_rms[:, None] * norm_gain[None, :]).astype(jnp.bfloat16)
    width_q = w_query.shape[1]
    width_k = w_key.shape[1]
    local_w = jnp.concatenate([w_query, w_key, w_value], 1)
    seqs, dps = lax.axis_size("seq"), lax.axis_size("dp")
    rows_w = local_w.shape[0]
    full_w = gather_blocks(local_w, cut_of(rows_w), ("seq", "dp"), 0)
    full_w = full_w.reshape(seqs * dps * rows_w, -1)
    projected = jnp.dot(normed, full_w, preferred_element_type=jnp.float32)
    start_row = lax.axis_index("seq") * row_count
    cosine, sine_part = angles(start_row + jnp.arange(row_count, dtype=jnp.int32), HD)
    d_out, slabs = attend_and_exchange(
        projected,
        cosine[:, 0],
        sine_part[:, 0],
        attn_grad[0],
        normed.T.reshape(seqs, dps, rows_w, row_count),
        3,
    )
    dnormed = lax.dot_general(
        d_out, full_w, (((1,), (1,)), ((), ())), preferred_element_type=jnp.float32
    )
    inner = jnp.sum(widened * norm_gain[None, :] * dnormed, -1).reshape(-1, 128)
    cotangents, parts, inners = gather_and_scatter(
        d_out, dnormed.astype(jnp.bfloat16), inner, cut_of(row_count), ("dp", "seq"), 2
    )
    grads = []
    for example in range(dps):
        grads.append(
            sum(
                jnp.dot(
                    slabs[example, s], cotangents[example, s], preferred_element_type=jnp.float32
                )
                for s in range(seqs)
            )
        )
    squares = jnp.stack([jnp.sum(grad * grad) for grad in grads])
    square_sum = total_of(jnp.broadcast_to(squares[:, None], (dps, 128)), 1)[:, 0]
    grad_rms = jnp.sqrt(square_sum / (D * (H + 2 * KVH) * HD) + EPSILON)
    factor = CLIP_BOUND / jnp.maximum(grad_rms, CLIP_BOUND)
    clipped = sum(factor[example] * grads[example] for example in range(dps))
    part_width = D // lax.axis_size("tensor")
    offset = lax.axis_index("tensor") * part_width
    part_grad = jnp.sum(parts.astype(jnp.float32), 0)
    gain_slab = lax.dynamic_slice_in_dim(norm_gain, offset, part_width, 0)
    input_slab = lax.dynamic_slice_in_dim(widened, offset, part_width, 1)
    scaled = gain_slab[None, :] * part_grad
    inner_sum = jnp.sum(inners, 0).reshape(row_count)
    mean_term = (inner_sum / D)[:, None]
    input_grad = (
        inverse_rms[:, None] * scaled
        - input_slab * (inverse_rms * inverse_rms * inverse_rms)[:, None] * mean_term
    )
    return (
        clipped[:, :width_q],
        clipped[:, width_q : width_q + width_k],
        clipped[:, width_q + width_k :],
        input_grad.astype(jnp.bfloat16)[None],
    )


def solution(mesh):
    return jax.shard_map(
        local,
        mesh=mesh,
        in_specs=(
            P("dp", "seq", None),
            P(("seq", "dp"), "tensor"),
            P(("seq", "dp"), "tensor"),
            P(("seq", "dp"), "tensor"),
            P(),
            P("dp", "seq", "tensor"),
        ),
        out_specs=(
            P(("seq", "dp"), "tensor"),
            P(("seq", "dp"), "tensor"),
            P(("seq", "dp"), "tensor"),
            P("dp", "seq", "tensor"),
        ),
        check_vma=False,
    )
```

```python
import functools
import math

import jax
import jax.numpy as jnp
from jax import lax
from jax.experimental import pallas as pl
from jax.experimental.pallas import tpu as pltpu
from jax.sharding import PartitionSpec as P

D = 3584
H = 8
KVH = 4
HD = 256
WINDOW = 256


EPSILON = 1e-06
SOFTCAP = 50.0
CLIP_BOUND = 1.0
ROPE_BASE = 10000.0


def angles(positions, head_width):
    frequency = ROPE_BASE ** (-2.0 * jnp.arange(head_width // 2).astype(jnp.float32) / head_width)
    phases = positions.astype(jnp.float32)[:, None] * frequency[None, :]
    return (jnp.cos(phases)[:, None, :], jnp.sin(phases)[:, None, :])


MESH = pl.DeviceIdType.MESH


def greet(axes, peers=()):
    barrier = pltpu.get_barrier_semaphore()
    for axis in axes:
        count = lax.axis_size(axis)
        me = lax.axis_index(axis)
        for step in (1, -1):

            @pl.when((me + step >= 0) & (me + step < count))
            def _():
                pl.semaphore_signal(
                    barrier, inc=1, device_id={axis: me + step}, device_id_type=MESH
                )

    for peer in peers:
        pl.semaphore_signal(barrier, inc=1, device_id=peer, device_id_type=MESH)
    near = len(peers)
    for axis in axes:
        me = lax.axis_index(axis)
        near = near + jnp.minimum(me, 1) + jnp.minimum(lax.axis_size(axis) - 1 - me, 1)
    pl.semaphore_wait(barrier, near)


class LineGather:
    def __init__(self, order, part, first, second, low, high, x_ref, out_ref, send_sem, recv_sem):
        self.order = order
        self.part, self.first, self.second = part, first, second
        self.rows = pl.ds(low, high - low)
        self.x_ref, self.out_ref = x_ref, out_ref
        self.send_sem, self.recv_sem = send_sem, recv_sem
        self.me = {axis: lax.axis_index(axis) for axis in (first, second)}
        self.count = {axis: lax.axis_size(axis) for axis in (first, second)}
        self.sends = []

    def slot(self, at):
        return self.out_ref.at[tuple(at[axis] for axis in self.order) + (self.rows,)]

    def copy(self, at, axis, step, own):
        way = (0 if axis == "seq" else 2) + (0 if step == 1 else 1)
        return pltpu.make_async_remote_copy(
            src_ref=self.x_ref.at[self.rows] if own else self.slot(at),
            dst_ref=self.slot(at),
            send_sem=self.send_sem.at[self.part, way, at["seq"], at["dp"]],
            recv_sem=self.recv_sem.at[self.part, at["seq"], at["dp"]],
            device_id={axis: self.me[axis] + step},
            device_id_type=MESH,
        )

    def inside(self, axis, value):
        return (value >= 0) & (value < self.count[axis])

    def send(self, at, axis, step, held, own=False):
        ok = held & self.inside(axis, self.me[axis] + step)

        @pl.when(ok)
        def _():
            self.copy(at, axis, step, own).start()

        self.sends.append((at, axis, step, ok, own))

    def receive(self, at, held):
        @pl.when(held)
        def _():
            self.copy(at, self.first, 1, False).wait_recv()

    def steps(self):
        first, second = self.first, self.second
        here = jnp.bool_(True)
        for axis in (first, second):
            for step in (1, -1):
                self.send(dict(self.me), axis, step, here, True)
        yield
        column = [(dict(self.me), here, True)]
        for hop in range(1, self.count[first]):
            for step in (1, -1):
                at = {**self.me, first: self.me[first] - step * hop}
                held = self.inside(first, at[first])
                self.receive(at, held)
                self.send(at, first, step, held)
                for way in (1, -1):
                    self.send(at, second, way, held)
                column.append((at, held, False))
            yield
        for hop in range(1, self.count[second]):
            for base, held_base, _ in column:
                for step in (1, -1):
                    at = {**base, second: self.me[second] - step * hop}
                    held = held_base & self.inside(second, at[second])
                    self.receive(at, held)
                    self.send(at, second, step, held)
            yield

    def finish(self):
        for at, axis, step, ok, own in self.sends:

            @pl.when(ok)
            def _():
                self.copy(at, axis, step, own).wait_send()


def run_gathers(gathers):
    live = [gather.steps() for gather in gathers]
    while live:
        still = []
        for walk in live:
            try:
                next(walk)
                still.append(walk)
            except StopIteration:
                pass
        live = still
    for gather in gathers:
        gather.finish()


def gather_kernel(cut, order, x_ref, out_ref, send_sem, recv_sem, own_sem):
    rows = x_ref.shape[0]
    own = pltpu.make_async_copy(
        x_ref, out_ref.at[tuple(lax.axis_index(axis) for axis in order)], own_sem
    )
    own.start()
    greet(("seq", "dp"))
    run_gathers(
        [
            LineGather(order, 0, "seq", "dp", 0, cut, x_ref, out_ref, send_sem, recv_sem),
            LineGather(order, 1, "dp", "seq", cut, rows, x_ref, out_ref, send_sem, recv_sem),
        ]
    )
    own.wait()


def gather_blocks(x, cut, order, collective_id):
    shape = (lax.axis_size("seq"), lax.axis_size("dp"))
    return pl.pallas_call(
        functools.partial(gather_kernel, cut, order),
        out_shape=jax.ShapeDtypeStruct(
            tuple(lax.axis_size(axis) for axis in order) + x.shape, x.dtype
        ),
        in_specs=[pl.BlockSpec(memory_space=pltpu.VMEM)],
        out_specs=pl.BlockSpec(memory_space=pl.ANY),
        scratch_shapes=[
            pltpu.SemaphoreType.DMA((2, 4) + shape),
            pltpu.SemaphoreType.DMA((2,) + shape),
            pltpu.SemaphoreType.DMA,
        ],
        compiler_params=pltpu.CompilerParams(
            collective_id=collective_id, has_side_effects=True
        ),
    )(x)


def tail_kernel(
    cut,
    order,
    x_ref,
    part_ref,
    inner_ref,
    block_ref,
    out_ref,
    parts_ref,
    inners_ref,
    blocks_ref,
    send_sem,
    recv_sem,
    own_sem,
    part_send,
    part_recv,
    inner_send,
    inner_recv,
    block_send,
    block_recv,
):
    rows = x_ref.shape[0]
    count, me = lax.axis_size("tensor"), lax.axis_index("tensor")
    width = part_ref.shape[1] // count

    def slab(index):
        return part_ref.at[:, pl.ds(pl.multiple_of(index * width, 128), width)]

    owns = [
        pltpu.make_async_copy(
            x_ref, out_ref.at[tuple(lax.axis_index(axis) for axis in order)], own_sem.at[0]
        ),
        pltpu.make_async_copy(slab(me), parts_ref.at[me], own_sem.at[1]),
        pltpu.make_async_copy(inner_ref, inners_ref.at[me], own_sem.at[2]),
        pltpu.make_async_copy(block_ref, blocks_ref.at[me], own_sem.at[3]),
    ]
    for own in owns:
        own.start()
    others = [lax.rem(me + hop, count) for hop in range(1, count)]
    greet(("seq", "dp"), [{"tensor": other} for other in others])
    copies = []
    for index, other in enumerate(others):
        copies.append(
            pltpu.make_async_remote_copy(
                src_ref=slab(other),
                dst_ref=parts_ref.at[me],
                send_sem=part_send.at[index],
                recv_sem=part_recv.at[index],
                device_id={"tensor": other},
                device_id_type=MESH,
            )
        )
        copies.append(
            pltpu.make_async_remote_copy(
                src_ref=inner_ref,
                dst_ref=inners_ref.at[me],
                send_sem=inner_send.at[index],
                recv_sem=inner_recv.at[index],
                device_id={"tensor": other},
                device_id_type=MESH,
            )
        )
    for index, other in enumerate(others):
        copies.append(
            pltpu.make_async_remote_copy(
                src_ref=block_ref,
                dst_ref=blocks_ref.at[me],
                send_sem=block_send.at[index],
                recv_sem=block_recv.at[index],
                device_id={"tensor": other},
                device_id_type=MESH,
            )
        )
    for copy in copies:
        copy.start()
    run_gathers(
        [
            LineGather(order, 0, "seq", "dp", 0, cut, x_ref, out_ref, send_sem, recv_sem),
            LineGather(order, 1, "dp", "seq", cut, rows, x_ref, out_ref, send_sem, recv_sem),
        ]
    )
    for copy in copies:
        copy.wait()
    for own in owns:
        own.wait()


def gather_and_scatter(x, part, inner, block, cut, order, collective_id):
    shape = (lax.axis_size("seq"), lax.axis_size("dp"))
    count = lax.axis_size("tensor")
    return pl.pallas_call(
        functools.partial(tail_kernel, cut, order),
        out_shape=(
            jax.ShapeDtypeStruct(tuple(lax.axis_size(axis) for axis in order) + x.shape, x.dtype),
            jax.ShapeDtypeStruct((count, part.shape[0], part.shape[1] // count), part.dtype),
            jax.ShapeDtypeStruct((count,) + inner.shape, inner.dtype),
            jax.ShapeDtypeStruct((count,) + block.shape, block.dtype),
        ),
        in_specs=[pl.BlockSpec(memory_space=pltpu.VMEM)] * 4,
        out_specs=(pl.BlockSpec(memory_space=pl.ANY),) * 4,
        scratch_shapes=[
            pltpu.SemaphoreType.DMA((2, 4) + shape),
            pltpu.SemaphoreType.DMA((2,) + shape),
            pltpu.SemaphoreType.DMA((4,)),
        ]
        + [pltpu.SemaphoreType.DMA((count - 1,))] * 6,
        compiler_params=pltpu.CompilerParams(
            collective_id=collective_id, has_side_effects=True
        ),
    )(x, part, inner, block)


def block_peers():
    seqs, dps = lax.axis_size("seq"), lax.axis_size("dp")
    mine = lax.axis_index("dp") * seqs + lax.axis_index("seq")
    others = [lax.rem(mine + hop, seqs * dps) for hop in range(1, seqs * dps)]
    return mine, [(other, lax.rem(other, seqs), other // seqs) for other in others]


def tensor_peers():
    count, me = lax.axis_size("tensor"), lax.axis_index("tensor")
    return [lax.rem(me + hop, count) for hop in range(1, count)]


class Exchange:
    def __init__(self, x_ref, out_ref, send_sem, recv_sem, own_sem):
        self.x_ref, self.out_ref = x_ref, out_ref
        self.send_sem, self.recv_sem, self.own_sem = send_sem, recv_sem, own_sem
        self.lanes, self.lane = lax.axis_size("tensor"), lax.axis_index("tensor")
        self.mine, self.peers = block_peers()
        self.sender = lax.rem(self.mine, self.lanes) == self.lane

    def copy(self, hop, slot):
        _, seq, dp = self.peers[hop]
        return pltpu.make_async_remote_copy(
            src_ref=self.x_ref.at[seq, dp],
            dst_ref=self.out_ref.at[slot],
            send_sem=self.send_sem.at[hop],
            recv_sem=self.recv_sem.at[slot],
            device_id={"seq": seq, "dp": dp},
            device_id_type=MESH,
        )

    def own(self):
        return pltpu.make_async_copy(
            self.x_ref.at[lax.axis_index("seq"), lax.axis_index("dp")],
            self.out_ref.at[self.mine // self.lanes],
            self.own_sem,
        )

    def start(self):
        @pl.when(self.sender)
        def _():
            for hop in range(len(self.peers)):
                self.copy(hop, self.mine // self.lanes).start()
            self.own().start()

    def finish(self):
        for slot in range((len(self.peers) + 1) // self.lanes):

            @pl.when(self.lane + slot * self.lanes != self.mine)
            def _():
                self.copy(0, slot).wait_recv()

        @pl.when(self.sender)
        def _():
            for hop in range(len(self.peers)):
                self.copy(hop, self.mine // self.lanes).wait_send()
            self.own().wait()


def exchange_semaphores():
    count, lanes = lax.axis_size("seq") * lax.axis_size("dp"), lax.axis_size("tensor")
    return [
        pltpu.SemaphoreType.DMA((count - 1,)),
        pltpu.SemaphoreType.DMA((count // lanes,)),
        pltpu.SemaphoreType.DMA,
    ]


def turn(vectors, cosine, sine_part, direction):
    half = vectors.shape[-1] // 2
    low, high = vectors[:, :half], vectors[:, half:]
    return jnp.concatenate(
        [
            low * cosine - direction * high * sine_part,
            high * cosine + direction * low * sine_part,
        ],
        -1,
    )


def product(left, right, left_dim, right_dim):
    return lax.dot_general(
        left, right, (((left_dim,), (right_dim,)), ((), ())), preferred_element_type=jnp.float32
    )


def attend_kernel(
    width_q,
    proj_ref,
    cos_ref,
    sin_ref,
    cot_ref,
    block_ref,
    out_ref,
    blocks_ref,
    held,
    before,
    back_out,
    back_in,
    own_grad,
    kv_sems,
    back_sems,
    *exchange_sems,
):
    rows = proj_ref.shape[0]
    width_k = (proj_ref.shape[1] - width_q) // 2
    heads_k = width_k // HD
    group = width_q // width_k
    inv_scale = 1.0 / math.sqrt(HD)
    seqs, seq = lax.axis_size("seq"), lax.axis_index("seq")
    cosine, sine_part = cos_ref[...], sin_ref[...]
    for head in range(heads_k):
        low = head * HD
        at = slice(low, low + HD)
        keys = proj_ref[:, width_q + low : width_q + low + HD]
        held[:, at] = turn(keys, cosine, sine_part, 1.0).astype(jnp.bfloat16)
        values = proj_ref[:, width_q + width_k + low : width_q + width_k + low + HD]
        held[:, width_k + low : width_k + low + HD] = values.astype(jnp.bfloat16)
    _, peers = block_peers()
    greet((), [{"seq": other, "dp": far} for _, other, far in peers])
    ahead = pltpu.make_async_remote_copy(
        src_ref=held,
        dst_ref=before,
        send_sem=kv_sems.at[0],
        recv_sem=kv_sems.at[1],
        device_id={"seq": seq + 1},
        device_id_type=MESH,
    )
    behind = pltpu.make_async_remote_copy(
        src_ref=back_out,
        dst_ref=back_in,
        send_sem=back_sems.at[0],
        recv_sem=back_sems.at[1],
        device_id={"seq": seq - 1},
        device_id_type=MESH,
    )
    has_next, has_last = seq < seqs - 1, seq > 0

    @pl.when(has_next)
    def _():
        ahead.start()

    exchange = Exchange(block_ref, blocks_ref, *exchange_sems)
    exchange.start()

    queries = []
    for head in range(heads_k * group):
        part = proj_ref[:, head * HD : (head + 1) * HD]
        queries.append(turn(part, cosine, sine_part, 1.0).astype(jnp.bfloat16))

    @pl.when(has_last)
    def _():
        ahead.wait_recv()

    @pl.when(jnp.logical_not(has_last))
    def _():
        before[...] = jnp.zeros_like(before)

    query_at = lax.broadcasted_iota(jnp.int32, (rows, rows), 0)
    key_at = lax.broadcasted_iota(jnp.int32, (rows, rows), 1)
    masks = (
        (key_at > query_at + (rows - WINDOW)) & (seq * rows - rows + key_at >= 0),
        (key_at <= query_at) & (key_at > query_at - WINDOW),
    )
    for head in range(heads_k):
        at = slice(head * HD, (head + 1) * HD)
        at_value = slice(width_k + head * HD, width_k + (head + 1) * HD)
        sides = (before, held)
        key_grads, value_grads = [0.0, 0.0], [0.0, 0.0]
        for member in range(group):
            index = head * group + member
            query = queries[index]
            cot = cot_ref[:, index * HD : (index + 1) * HD]
            squashes, terms, slopes = [], [], []
            for side, mask in zip(sides, masks):
                squash = jnp.tanh(product(query, side[:, at], 1, 1) * inv_scale / SOFTCAP)
                squashes.append(squash)
                terms.append(jnp.where(mask, jnp.exp(SOFTCAP * squash), 0.0))
                slopes.append(product(cot, side[:, at_value], 1, 1))
            total = sum(jnp.sum(term, -1, keepdims=True) for term in terms)
            probs = [term / total for term in terms]
            delta = sum(
                jnp.sum(prob * slope, -1, keepdims=True) for prob, slope in zip(probs, slopes)
            )
            dquery = 0.0
            for which in range(2):
                prob, squash = probs[which], squashes[which]
                dlogits = (
                    prob * (slopes[which] - delta) * (1.0 - squash * squash) * inv_scale
                ).astype(jnp.bfloat16)
                dquery = dquery + product(dlogits, sides[which][:, at], 1, 0)
                key_grads[which] = key_grads[which] + product(dlogits, query, 0, 0)
                value_grads[which] = value_grads[which] + product(
                    prob.astype(jnp.bfloat16), cot, 0, 0
                )
            out_ref[:, index * HD : (index + 1) * HD] = turn(
                dquery, cosine, sine_part, -1.0
            ).astype(jnp.bfloat16)
        back_out[:, at] = key_grads[0].astype(jnp.bfloat16)
        back_out[:, at_value] = value_grads[0].astype(jnp.bfloat16)
        own_grad[:, at] = key_grads[1]
        own_grad[:, at_value] = value_grads[1]

    @pl.when(has_last)
    def _():
        behind.start()

    @pl.when(has_next)
    def _():
        behind.wait_recv()
        own_grad[...] += back_in[...].astype(jnp.float32)

    for head in range(heads_k):
        at = slice(head * HD, (head + 1) * HD)
        out_ref[:, width_q + head * HD : width_q + (head + 1) * HD] = turn(
            own_grad[:, at], cosine, sine_part, -1.0
        ).astype(jnp.bfloat16)
    out_ref[:, width_q + width_k :] = own_grad[:, width_k:].astype(jnp.bfloat16)

    @pl.when(has_next)
    def _():
        ahead.wait_send()

    @pl.when(has_last)
    def _():
        behind.wait_send()

    exchange.finish()


def attend_and_exchange(projected, cosine, sine_part, cotangent, blocks, collective_id):
    rows, width_q = cotangent.shape
    width_k = (projected.shape[1] - width_q) // 2
    return pl.pallas_call(
        functools.partial(attend_kernel, width_q),
        out_shape=(
            jax.ShapeDtypeStruct(projected.shape, jnp.bfloat16),
            jax.ShapeDtypeStruct(
                (blocks.shape[0] * blocks.shape[1] // lax.axis_size("tensor"),)
                + blocks.shape[2:],
                blocks.dtype,
            ),
        ),
        in_specs=[pl.BlockSpec(memory_space=pltpu.VMEM)] * 5,
        out_specs=(pl.BlockSpec(memory_space=pltpu.VMEM), pl.BlockSpec(memory_space=pl.ANY)),
        scratch_shapes=[
            pltpu.VMEM((rows, 2 * width_k), jnp.bfloat16),
            pltpu.VMEM((rows, 2 * width_k), jnp.bfloat16),
            pltpu.VMEM((rows, 2 * width_k), jnp.bfloat16),
            pltpu.VMEM((rows, 2 * width_k), jnp.bfloat16),
            pltpu.VMEM((rows, 2 * width_k), jnp.float32),
            pltpu.SemaphoreType.DMA((2,)),
            pltpu.SemaphoreType.DMA((2,)),
        ]
        + exchange_semaphores(),
        compiler_params=pltpu.CompilerParams(
            collective_id=collective_id, has_side_effects=True
        ),
    )(projected, cosine, sine_part, cotangent, blocks)


def total_kernel(x_ref, out_ref, held, send_sem, recv_sem, send_wide, recv_wide, own_sem):
    mine, peers = block_peers()
    lane = lax.axis_index("tensor")
    others = tensor_peers()
    own = pltpu.make_async_copy(x_ref, held.at[lane, mine], own_sem)
    own.start()
    greet(
        (),
        [{"seq": seq, "dp": dp} for _, seq, dp in peers] + [{"tensor": other} for other in others],
    )
    near = [
        pltpu.make_async_remote_copy(
            src_ref=x_ref,
            dst_ref=held.at[lane, mine],
            send_sem=send_sem.at[hop],
            recv_sem=recv_sem.at[mine],
            device_id={"seq": seq, "dp": dp},
            device_id_type=MESH,
        )
        for hop, (_, seq, dp) in enumerate(peers)
    ]
    for copy in near:
        copy.start()
    for index, seq, dp in peers:
        pltpu.make_async_remote_copy(
            src_ref=x_ref,
            dst_ref=held.at[lane, index],
            send_sem=send_sem.at[0],
            recv_sem=recv_sem.at[index],
            device_id={"seq": seq, "dp": dp},
            device_id_type=MESH,
        ).wait_recv()
    own.wait()
    far = [
        pltpu.make_async_remote_copy(
            src_ref=held.at[lane],
            dst_ref=held.at[lane],
            send_sem=send_wide.at[hop],
            recv_sem=recv_wide.at[hop],
            device_id={"tensor": other},
            device_id_type=MESH,
        )
        for hop, other in enumerate(others)
    ]
    for copy in far:
        copy.start()
    for copy in far:
        copy.wait()
    for copy in near:
        copy.wait_send()
    out_ref[...] = jnp.sum(held[...], (0, 1))


def total_of(x, collective_id):
    count, lanes = lax.axis_size("seq") * lax.axis_size("dp"), lax.axis_size("tensor")
    return pl.pallas_call(
        total_kernel,
        out_shape=jax.ShapeDtypeStruct(x.shape, x.dtype),
        in_specs=[pl.BlockSpec(memory_space=pltpu.VMEM)],
        out_specs=pl.BlockSpec(memory_space=pltpu.VMEM),
        scratch_shapes=[
            pltpu.VMEM((lanes, count) + x.shape, x.dtype),
            pltpu.SemaphoreType.DMA((count - 1,)),
            pltpu.SemaphoreType.DMA((count,)),
            pltpu.SemaphoreType.DMA((lanes - 1,)),
            pltpu.SemaphoreType.DMA((lanes - 1,)),
            pltpu.SemaphoreType.DMA,
        ],
        compiler_params=pltpu.CompilerParams(
            collective_id=collective_id, has_side_effects=True
        ),
    )(x)


def cut_of(rows):
    return max(16, rows // 7 // 16 * 16)


def local(inputs, w_query, w_key, w_value, norm_gain, attn_grad):
    widened = inputs[0].astype(jnp.float32)
    row_count = widened.shape[0]
    inverse_rms = lax.rsqrt(jnp.mean(widened * widened, -1) + EPSILON)
    normed = (widened * inverse_rms[:, None] * norm_gain[None, :]).astype(jnp.bfloat16)
    width_q = w_query.shape[1]
    width_k = w_key.shape[1]
    local_w = jnp.concatenate([w_query, w_key, w_value], 1)
    seqs, dps = lax.axis_size("seq"), lax.axis_size("dp")
    rows_w = local_w.shape[0]
    full_w = gather_blocks(local_w, cut_of(rows_w), ("seq", "dp"), 0)
    full_w = full_w.reshape(seqs * dps * rows_w, -1)
    projected = jnp.dot(normed, full_w, preferred_element_type=jnp.float32)
    start_row = lax.axis_index("seq") * row_count
    cosine, sine_part = angles(start_row + jnp.arange(row_count, dtype=jnp.int32), HD)
    d_out, passed = attend_and_exchange(
        projected,
        cosine[:, 0],
        sine_part[:, 0],
        attn_grad[0],
        normed.T.reshape(seqs, dps, rows_w, row_count),
        3,
    )
    dnormed = lax.dot_general(
        d_out, full_w, (((1,), (1,)), ((), ())), preferred_element_type=jnp.float32
    )
    inner = jnp.sum(widened * norm_gain[None, :] * dnormed, -1).reshape(-1, 128)
    cotangents, parts, inners, slabs = gather_and_scatter(
        d_out, dnormed.astype(jnp.bfloat16), inner, passed, cut_of(row_count), ("dp", "seq"), 2
    )
    grads = []
    lanes = lax.axis_size("tensor")
    for example in range(dps):
        grads.append(
            sum(
                jnp.dot(
                    slabs[(example * seqs + s) % lanes, (example * seqs + s) // lanes],
                    cotangents[example, s],
                    preferred_element_type=jnp.float32
                )
                for s in range(seqs)
            )
        )
    squares = jnp.stack([jnp.sum(grad * grad) for grad in grads])
    square_sum = total_of(jnp.broadcast_to(squares[:, None], (dps, 128)), 1)[:, 0]
    grad_rms = jnp.sqrt(square_sum / (D * (H + 2 * KVH) * HD) + EPSILON)
    factor = CLIP_BOUND / jnp.maximum(grad_rms, CLIP_BOUND)
    clipped = sum(factor[example] * grads[example] for example in range(dps))
    part_width = D // lax.axis_size("tensor")
    offset = lax.axis_index("tensor") * part_width
    part_grad = jnp.sum(parts.astype(jnp.float32), 0)
    gain_slab = lax.dynamic_slice_in_dim(norm_gain, offset, part_width, 0)
    input_slab = lax.dynamic_slice_in_dim(widened, offset, part_width, 1)
    scaled = gain_slab[None, :] * part_grad
    inner_sum = jnp.sum(inners, 0).reshape(row_count)
    mean_term = (inner_sum / D)[:, None]
    input_grad = (
        inverse_rms[:, None] * scaled
        - input_slab * (inverse_rms * inverse_rms * inverse_rms)[:, None] * mean_term
    )
    return (
        clipped[:, :width_q],
        clipped[:, width_q : width_q + width_k],
        clipped[:, width_q + width_k :],
        input_grad.astype(jnp.bfloat16)[None],
    )


def solution(mesh):
    return jax.shard_map(
        local,
        mesh=mesh,
        in_specs=(
            P("dp", "seq", None),
            P(("seq", "dp"), "tensor"),
            P(("seq", "dp"), "tensor"),
            P(("seq", "dp"), "tensor"),
            P(),
            P("dp", "seq", "tensor"),
        ),
        out_specs=(
            P(("seq", "dp"), "tensor"),
            P(("seq", "dp"), "tensor"),
            P(("seq", "dp"), "tensor"),
            P("dp", "seq", "tensor"),
        ),
        check_vma=False,
    )
```
